128 devices in a mesh: rows: 2 (over core), cols: 64 (over z, y, x).
Axes of the slice: x: 4, y: 4, z: 4, core: 2. Of those that a mesh axis runs over, the one named last changes fastest.
Arguments:
- jacobian: float32 [32768, 16384], P('rows', 'cols'), may hold values from -0.046875 to 0.046875
- targets: float32 [64, 32768], P(None, 'rows'), may hold values from 0 to 1
- anchor: float32 [64, 16384], P(None, 'cols'), may hold values from -6 to 6
- precision: float32 [16384], P('cols'), may hold values from 0.3 to 3
Outputs:
- samples: float32 [64, 16384], P(None, 'cols')
The draws below stay inside these ranges and needn't reach their ends.
All inputs are finite; a program needn't handle non-finite values.
Results may differ from the reference program's by a relative error of at most 0.0001.
Values sent between devices are 32-bit elements; how exact they have to be, the bound alone decides.
No kernel may reach another device: no remote copies, remote signals or barrier semaphores. Data moves between devices by JAX's collectives and lax.ppermute only.
A program may use at most 128 MiB of HBM per device.

```python
import math
import jax
import jax.numpy as jnp
from jax import lax

PARAMS = 16384
SAMPLES = 64
STEPS = 3
ROWS = 32768


def block_scale(rng, dims, cuts, least, top_value):
    level, own = 1.0, jax.random.fold_in(rng, 6)
    for axis_at, shards_of in cuts:
        heights = jnp.exp(jax.random.uniform(jax.random.fold_in(own, axis_at), (shards_of,), jnp.float32, least / len(cuts), top_value / len(cuts)))
        level = level * jnp.repeat(heights, dims[axis_at] // shards_of).reshape([-1 if axis == axis_at else 1 for axis in range(len(dims))])
    return level


def gaussian(stream_key, extent, scale, limit, cuts=(), dtype=jnp.bfloat16):
    values = jax.random.normal(stream_key, extent, jnp.float32) * scale
    if len(cuts) > 0:
        values = block_scale(stream_key, extent, cuts, -0.22, 0.18) * values
    return jnp.clip(values, min=-limit, max=limit).astype(dtype)


def setup_inputs(seed: int = 0) -> dict:
    splits = jax.random.split(jax.random.key(seed), 5)
    jacobian = gaussian(splits[0], (ROWS, PARAMS), PARAMS ** -0.5, 0.046875, ((0, 2), (1, 64)), jnp.float32)
    targets = jnp.clip(1.0 * jax.random.uniform(splits[1], (SAMPLES, ROWS), jnp.float32) ** block_scale(splits[1], (SAMPLES, ROWS), ((1, 2),), -0.2, 0.2), 0.0, 1.0)
    anchor = gaussian(splits[2], (SAMPLES, PARAMS), 1.0, 6.0, ((1, 64),), jnp.float32)
    precision = jnp.clip(jnp.exp(math.log(3.0) - 2.3025851 * jax.random.uniform(splits[3], (PARAMS,), jnp.float32) ** block_scale(splits[3], (PARAMS,), ((0, 64),), -0.2, 0.2)), 0.3, 3.0)
    return dict(jacobian=jacobian, targets=targets, anchor=anchor, precision=precision)


def reference(jacobian, targets, anchor, precision):
    clip_level = 0.2 * math.sqrt(ROWS / PARAMS)
    theta = anchor
    velocity = jnp.zeros_like(anchor)
    for step in range(STEPS):
        logits = lax.dot_general(theta, jacobian, (((1,), (1,)), ((), ())), precision=lax.Precision.HIGHEST, preferred_element_type=jnp.float32)
        residual = jax.nn.sigmoid(logits) - targets
        gradient = jnp.dot(residual, jacobian, precision=lax.Precision.HIGHEST, preferred_element_type=jnp.float32)
        gradient = gradient + precision[None, :] * (theta - anchor)
        rms_value = jnp.sqrt(lax.optimization_barrier(jnp.sum(gradient * gradient, axis=1)) / PARAMS + 1e-06)
        scale = jnp.minimum(1.0, clip_level / rms_value)
        velocity = 0.9 * velocity + scale[:, None] * gradient
        theta = theta - 0.5 * velocity
    return theta
```

```python
import math

import jax
import jax.numpy as jnp
from jax import lax
from jax.sharding import Mesh
from jax.sharding import PartitionSpec as P

STEPS = 3
SIDE = 4
CUBE = 8
SHIFT = (0, 1, 1)
AXES = ("rows", "z", "y", "x")
COLS = ("z", "y", "x")


def place(core, at):
    turned = [(p + core + s) % SIDE for p, s in zip(at, SHIFT)]
    half = [(t + 1) // 2 % 2 for t in turned]
    pair = [t // 2 for t in turned]
    return half[0] * 4 + half[1] * 2 + half[2], pair[0] * 4 + pair[1] * 2 + pair[2]


def cube_groups():
    first, second = {}, {}
    for device in range(2 * SIDE**3):
        core, z, y, x = device // 64, device // 16 % 4, device // 4 % 4, device % 4
        half, pair = place(core, (z, y, x))
        first.setdefault((core, pair), {})[half] = device
        second.setdefault((core, half), {})[pair] = device
    in_order = lambda groups: [[group[k] for k in range(CUBE)] for _, group in sorted(groups.items())]
    return in_order(first), in_order(second)


FIRST, SECOND = cube_groups()


def exchange(x, groups):
    return lax.all_to_all(x, AXES, split_axis=0, concat_axis=0, axis_index_groups=groups, tiled=True)


def copies(x, n):
    return jnp.broadcast_to(x[None], (n, *x.shape))


def own_block():
    return place(lax.axis_index("rows"), [lax.axis_index(a) for a in COLS])


def product(theta, jacobian):
    return lax.dot_general(
        theta,
        jacobian,
        (((1,), (1,)), ((), ())),
        precision=lax.Precision.HIGHEST,
        preferred_element_type=jnp.float32,
    )


def body(jacobian, targets, anchor, precision):
    samples, col_dev = anchor.shape
    row_dev = jacobian.shape[0]
    part = row_dev // CUBE
    block = part // CUBE
    total_params = col_dev * SIDE**3
    clip_level = 0.2 * math.sqrt(row_dev * 2 / total_params)
    half, pair = own_block()
    own_targets = lax.dynamic_slice(targets, (0, half * part + pair * block), (samples, block))

    def summed(x, square):
        parts = jnp.swapaxes(x.reshape(samples, CUBE, part), 0, 1)
        tail = jnp.broadcast_to(square[None, :, None], (CUBE, samples, 128))
        got = jnp.sum(exchange(jnp.concatenate([parts, tail], 2), FIRST), axis=0)
        blocks = jnp.swapaxes(got[:, :part].reshape(samples, CUBE, block), 0, 1)
        tail = jnp.broadcast_to(got[None, :, part:], (CUBE, samples, 128))
        got = jnp.sum(exchange(jnp.concatenate([blocks, tail], 2), SECOND), axis=0)
        return got[:, :block], got[:, block]

    def spread(x):
        got = exchange(copies(x, CUBE), SECOND)
        got = exchange(copies(got, CUBE), FIRST)
        return jnp.swapaxes(got.reshape(CUBE * CUBE, samples, block), 0, 1).reshape(samples, row_dev)

    def scale_of(squares):
        return jnp.minimum(1.0, clip_level / jnp.sqrt(squares / total_params + 1e-06))[:, None]

    theta = anchor
    velocity = jnp.zeros_like(anchor)
    logits, _ = summed(product(anchor, jacobian), jnp.zeros((samples,), jnp.float32))
    slope = jnp.zeros_like(logits)
    for step in range(STEPS):
        residual = spread(jax.nn.sigmoid(logits) - own_targets)
        gradient = jnp.dot(
            residual, jacobian, precision=lax.Precision.HIGHEST, preferred_element_type=jnp.float32
        )
        gradient = gradient + lax.ppermute(gradient, "rows", [(0, 1), (1, 0)])
        gradient = gradient + precision[None, :] * (theta - anchor)
        square = jnp.sum(gradient * gradient, axis=1)
        if step + 1 < STEPS:
            moved, squares = summed(product(gradient, jacobian), square)
            scale = scale_of(squares)
            slope = 0.9 * slope + scale * moved
            logits = logits - 0.5 * slope
        else:
            everything = lax.all_to_all(copies(square, SIDE**3), COLS, split_axis=0, concat_axis=0, tiled=True)
            scale = scale_of(jnp.sum(everything, axis=0))
        velocity = 0.9 * velocity + scale * gradient
        theta = theta - 0.5 * velocity
    return theta


def solution(mesh):
    cubes = Mesh(mesh.devices.reshape(2, SIDE, SIDE, SIDE), AXES)
    in_specs = (P("rows", COLS), P(None, "rows"), P(None, COLS), P(COLS))
    out_specs = P(None, COLS)
    return jax.shard_map(body, mesh=cubes, in_specs=in_specs, out_specs=out_specs, check_vma=False)
```

```python
import math

import jax
import jax.numpy as jnp
from jax import lax
from jax.experimental import pallas as pl
from jax.experimental.pallas import tpu as pltpu
from jax.sharding import Mesh
from jax.sharding import PartitionSpec as P

STEPS = 3
SIDE = 4
CUBE = 8
SHIFT = (0, 1, 1)
AXES = ("rows", "z", "y", "x")
COLS = ("z", "y", "x")
LANES = 128
TAIL = 8
F32 = jnp.float32
BF16 = jnp.bfloat16
ACROSS = (((1,), (1,)), ((), ()))
DOWN = (((1,), (0,)), ((), ()))
WHOLE = pl.BlockSpec(memory_space=pltpu.VMEM)


def place(core, at):
    turned = [(p + core + s) & (SIDE - 1) for p, s in zip(at, SHIFT)]
    half = [((t + 1) >> 1) & 1 for t in turned]
    pair = [t >> 1 for t in turned]
    return half[0] * 4 + half[1] * 2 + half[2], pair[0] * 4 + pair[1] * 2 + pair[2]


def cube_groups():
    first, second = {}, {}
    for device in range(2 * SIDE**3):
        core, z, y, x = device // 64, device // 16 % 4, device // 4 % 4, device % 4
        half, pair = place(core, (z, y, x))
        first.setdefault((core, pair), {})[half] = device
        second.setdefault((core, half), {})[pair] = device
    in_order = lambda groups: [[group[k] for k in range(CUBE)] for _, group in sorted(groups.items())]
    return in_order(first), in_order(second)


FIRST, SECOND = cube_groups()


def exchange(x, groups):
    return lax.all_to_all(x, AXES, split_axis=0, concat_axis=0, axis_index_groups=groups, tiled=True)


def own_block():
    return place(lax.axis_index("rows"), [lax.axis_index(a) for a in COLS])


def call(kernel, out_shape, name, mib, **kw):
    return pl.pallas_call(
        kernel,
        out_shape=out_shape,
        name=name,
        compiler_params=pltpu.CompilerParams(vmem_limit_bytes=mib << 20),
        **kw,
    )


def array(*shape, dtype=F32):
    return jax.ShapeDtypeStruct(shape, dtype)


def halves(x):
    high = x.astype(BF16)
    return high, (x - high.astype(F32)).astype(BF16)


def dot(a, b, dims):
    return lax.dot_general(a, b, dims, preferred_element_type=F32)


def diagonal(samples):
    shape = (samples, LANES)
    return lax.broadcasted_iota(jnp.int32, shape, 0) == lax.broadcasted_iota(jnp.int32, shape, 1)


def to_lanes(column):
    samples = column.shape[0]
    row = jnp.sum(jnp.where(diagonal(samples), column, 0.0), axis=0, keepdims=True)
    return jnp.broadcast_to(row, (TAIL, LANES))


def to_column(row, samples):
    return jnp.sum(jnp.where(diagonal(samples), row, 0.0), axis=1, keepdims=True)


def stacked(x):
    high, low = halves(x)
    return jnp.concatenate([high, low], 0), high


def put_part(out_ref, at, both, high, jac_high, jac_low, tail):
    samples = high.shape[0]
    wide = dot(both, jac_high, ACROSS)
    logits = wide[:samples] + wide[samples:] + dot(high, jac_low, ACROSS)
    tiles = logits.shape[1] // LANES
    for t in range(tiles):
        out_ref[at, t * samples : (t + 1) * samples] = logits[:, t * LANES : (t + 1) * LANES]
    out_ref[at, tiles * samples :] = tail


def open_kernel(at_ref, anchor_ref, targets_ref, jac_ref, out_ref, own_ref, high_ref, low_ref):
    part = jac_ref.shape[0]
    samples = targets_ref.shape[0]
    for t in range(targets_ref.shape[1] // LANES):
        own_ref[t * samples : (t + 1) * samples] = targets_ref[:, t * LANES : (t + 1) * LANES]
    jac_high, jac_low = halves(jac_ref[...])
    rows = pl.ds(pl.multiple_of(pl.program_id(0) * part, part), part)
    high_ref[rows] = jac_high
    low_ref[rows] = jac_low
    both, high = stacked(anchor_ref[...])
    put_part(out_ref, 0, both, high, jac_high, jac_low, jnp.zeros((TAIL, LANES), F32))


def opened(at, anchor, targets, jacobian):
    samples, cols = anchor.shape
    rows = jacobian.shape[0]
    part = rows // CUBE
    block = part // CUBE
    length = part // LANES * samples + TAIL
    return pl.pallas_call(
        open_kernel,
        name="opened",
        out_shape=[
            array(CUBE, length, LANES),
            array(block // LANES * samples, LANES),
            array(rows, cols, dtype=BF16),
            array(rows, cols, dtype=BF16),
        ],
        grid_spec=pltpu.PrefetchScalarGridSpec(
            num_scalar_prefetch=1,
            grid=(CUBE,),
            in_specs=[
                pl.BlockSpec((samples, cols), lambda i, at: (0, 0)),
                pl.BlockSpec((samples, block), lambda i, at: (0, at[0])),
                pl.BlockSpec((part, cols), lambda i, at: (i, 0)),
            ],
            out_specs=[
                pl.BlockSpec((1, length, LANES), lambda i, at: (i, 0, 0)),
                pl.BlockSpec((block // LANES * samples, LANES), lambda i, at: (0, 0)),
                WHOLE,
                WHOLE,
            ],
        ),
        compiler_params=pltpu.CompilerParams(vmem_limit_bytes=16 << 20),
    )(at, anchor, in_hbm(targets), in_hbm(jacobian))


def in_hbm(x):
    return pltpu.with_memory_space_constraint(x, pltpu.HBM)


def part_sum_kernel(in_ref, out_ref):
    length = out_ref.shape[1] - TAIL
    body = CUBE * length
    for i in range(CUBE):
        out_ref[i, :length] = jnp.sum(in_ref[:, i * length : (i + 1) * length], axis=0)
    tail = jnp.sum(in_ref[:, body:], axis=0)
    for i in range(CUBE):
        out_ref[i, length:] = tail


def part_sum(parts):
    length = (parts.shape[1] - TAIL) // CUBE + TAIL
    return call(
        part_sum_kernel, array(CUBE, length, LANES), "part_sum", 4, in_specs=[WHOLE], out_specs=WHOLE
    )(parts)


def scale_from(row, samples, clip_level, params):
    squares = to_column(row, samples)
    return jnp.minimum(1.0, clip_level / jnp.sqrt(squares / params + 1e-06))


def residual_to(out_ref, logits, targets):
    residual = jax.nn.sigmoid(logits) - targets
    for i in range(CUBE):
        out_ref[i] = residual


def first_residual_kernel(in_ref, targets_ref, residual_ref, logits_ref):
    logits = jnp.sum(in_ref[:, : targets_ref.shape[0]], axis=0)
    logits_ref[...] = logits
    residual_to(residual_ref, logits, targets_ref[...])


def first_residual(parts, targets):
    return call(
        first_residual_kernel,
        [array(CUBE, *targets.shape), array(*targets.shape)],
        "first_residual",
        4,
        in_specs=[WHOLE] * 2,
        out_specs=[WHOLE] * 2,
    )(parts, targets)


def next_residual(parts, targets, logits, slope, samples, clip_level, params):
    def kernel(in_ref, targets_ref, logits_ref, slope_ref, residual_ref, out_logits_ref, out_slope_ref, scale_ref):
        length = targets_ref.shape[0]
        row = jnp.sum(in_ref[:, length:], axis=0)[:1]
        scale = scale_from(row, samples, clip_level, params)
        scale_ref[...] = jnp.broadcast_to(scale, scale_ref.shape)
        moved = jnp.sum(in_ref[:, :length], axis=0)
        for t in range(length // samples):
            at = slice(t * samples, (t + 1) * samples)
            out_slope_ref[at] = 0.9 * slope_ref[at] + scale * moved[at]
        logits = logits_ref[...] - 0.5 * out_slope_ref[...]
        out_logits_ref[...] = logits
        residual_to(residual_ref, logits, targets_ref[...])

    shape = targets.shape
    return call(
        kernel,
        [array(CUBE, *shape), array(*shape), array(*shape), array(samples, LANES)],
        "next_residual",
        4,
        in_specs=[WHOLE] * 4,
        out_specs=[WHOLE] * 4,
    )(parts, targets, logits, slope)


def gradient_kernel(residual_ref, high_ref, low_ref, out_ref):
    samples, cols = out_ref.shape
    blocks, length, _ = residual_ref.shape
    tiles = length // samples
    rows = tiles * LANES
    wide = jnp.zeros((2 * samples, cols), F32)
    narrow = jnp.zeros((samples, cols), F32)
    for c in range(0, blocks, CUBE):
        block = [
            residual_ref[b, t * samples : (t + 1) * samples] for b in range(c, c + CUBE) for t in range(tiles)
        ]
        both, high = stacked(jnp.concatenate(block, 1))
        at = slice(c * rows, (c + CUBE) * rows)
        wide += dot(both, high_ref[at], DOWN)
        narrow += dot(high, low_ref[at], DOWN)
    out_ref[...] = wide[:samples] + wide[samples:] + narrow


def gradient_part(residual, high, low, samples):
    return call(
        gradient_kernel,
        array(samples, high.shape[1]),
        "gradient",
        16,
        in_specs=[WHOLE] * 3,
        out_specs=WHOLE,
    )(residual, high, low)


def moved_on(state):
    theta_ref, velocity_ref, gradient_ref, scale_ref = state
    velocity = 0.9 * velocity_ref[...] + scale_ref[:, :1] * gradient_ref[...]
    return theta_ref[...] - 0.5 * velocity, velocity


def whole_gradient(own_ref, other_ref, prec_ref, anchor_ref, theta):
    gradient = own_ref[...] + other_ref[...] + prec_ref[...] * (theta - anchor_ref[...])
    return gradient, jnp.sum(gradient * gradient, axis=1, keepdims=True)


def push_parts(out_ref, gradient, square, high_ref, low_ref):
    both, high = stacked(gradient)
    tail = to_lanes(square)
    part = high_ref.shape[0] // CUBE
    for j in range(CUBE):
        at = slice(j * part, (j + 1) * part)
        put_part(out_ref, j, both, high, high_ref[at], low_ref[at], tail)


def first_push_kernel(own_ref, other_ref, prec_ref, anchor_ref, high_ref, low_ref, out_ref, gradient_ref):
    gradient, square = whole_gradient(own_ref, other_ref, prec_ref, anchor_ref, anchor_ref[...])
    gradient_ref[...] = gradient
    push_parts(out_ref, gradient, square, high_ref, low_ref)


def next_push_kernel(own_ref, other_ref, prec_ref, anchor_ref, high_ref, low_ref, *refs):
    state, (out_ref, gradient_ref, theta_ref, velocity_ref) = refs[:4], refs[4:]
    theta, velocity = moved_on(state)
    theta_ref[...] = theta
    velocity_ref[...] = velocity
    gradient, square = whole_gradient(own_ref, other_ref, prec_ref, anchor_ref, theta)
    gradient_ref[...] = gradient
    push_parts(out_ref, gradient, square, high_ref, low_ref)


def pushed(own, other, prec, anchor, high, low, state=()):
    samples, cols = anchor.shape
    length = high.shape[0] // CUBE // LANES * samples + TAIL
    outs = 3 if state else 1
    return call(
        next_push_kernel if state else first_push_kernel,
        [array(CUBE, length, LANES)] + [array(samples, cols)] * outs,
        "next_push" if state else "first_push",
        16,
        in_specs=[WHOLE] * (6 + len(state)),
        out_specs=[WHOLE] * (1 + outs),
    )(own, other, prec, anchor, high, low, *state)


def last_kernel(own_ref, other_ref, prec_ref, anchor_ref, *refs):
    state, (squares_ref, gradient_ref, theta_ref, velocity_ref) = refs[:4], refs[4:]
    theta, velocity = moved_on(state)
    theta_ref[...] = theta
    velocity_ref[...] = velocity
    gradient, square = whole_gradient(own_ref, other_ref, prec_ref, anchor_ref, theta)
    gradient_ref[...] = gradient
    squares_ref[...] = jnp.broadcast_to(to_lanes(square)[:1], squares_ref.shape)


def last_gradient(own, other, prec, anchor, state):
    shape = anchor.shape
    return call(
        last_kernel,
        [array(SIDE**3, LANES)] + [array(*shape)] * 3,
        "last_gradient",
        4,
        in_specs=[WHOLE] * 8,
        out_specs=[WHOLE] * 4,
    )(own, other, prec, anchor, *state)


def close(squares, theta, velocity, gradient, clip_level, params):
    samples = theta.shape[0]

    def kernel(squares_ref, theta_ref, velocity_ref, gradient_ref, out_ref):
        row = jnp.sum(squares_ref[...], axis=0, keepdims=True)
        scale = scale_from(row, samples, clip_level, params)
        velocity = 0.9 * velocity_ref[...] + scale * gradient_ref[...]
        out_ref[...] = theta_ref[...] - 0.5 * velocity

    return call(kernel, array(*theta.shape), "close", 4, in_specs=[WHOLE] * 4, out_specs=WHOLE)(
        squares, theta, velocity, gradient
    )


def body(jacobian, targets, anchor, precision):
    samples, col_dev = anchor.shape
    row_dev = jacobian.shape[0]
    params = col_dev * SIDE**3
    clip_level = 0.2 * math.sqrt(row_dev * 2 / params)
    half, pair = own_block()
    at = jnp.reshape(half * CUBE + pair, (1,)).astype(jnp.int32)
    prec = precision[None, :]

    def summed(parts):
        return exchange(part_sum(exchange(parts, FIRST)), SECOND)

    def spread(residual):
        got = exchange(residual, SECOND)
        got = exchange(jnp.broadcast_to(got[None], (CUBE, *got.shape)), FIRST)
        return got.reshape(CUBE**2, *residual.shape[1:])

    parts, own, high, low = opened(at, anchor, targets, jacobian)
    residual, logits = first_residual(summed(parts), own)
    slope = jnp.zeros_like(logits)
    state = ()
    for step in range(STEPS):
        gradient = gradient_part(spread(residual), high, low, samples)
        other = lax.ppermute(gradient, "rows", [(0, 1), (1, 0)])
        if step + 1 == STEPS:
            break
        parts, gradient, *moved = pushed(gradient, other, prec, anchor, high, low, state)
        theta, velocity = moved if moved else (anchor, jnp.zeros_like(anchor))
        residual, logits, slope, scale = next_residual(
            summed(parts), own, logits, slope, samples, clip_level, params
        )
        state = (theta, velocity, gradient, scale)
    squares, gradient, theta, velocity = last_gradient(gradient, other, prec, anchor, state)
    squares = lax.all_to_all(squares, COLS, split_axis=0, concat_axis=0, tiled=True)
    return close(squares, theta, velocity, gradient, clip_level, params)


def solution(mesh):
    cubes = Mesh(mesh.devices.reshape(2, SIDE, SIDE, SIDE), AXES)
    in_specs = (P("rows", COLS), P(None, "rows"), P(None, COLS), P(COLS))
    out_specs = P(None, COLS)
    return jax.shard_map(body, mesh=cubes, in_specs=in_specs, out_specs=out_specs, check_vma=False)
```

```python
import math

import jax
import jax.numpy as jnp
from jax import lax
from jax.experimental import pallas as pl
from jax.experimental.pallas import tpu as pltpu
from jax.sharding import Mesh
from jax.sharding import PartitionSpec as P

STEPS = 3
SIDE = 4
CUBE = 8
SHIFT = (0, 1, 1)
AXES = ("rows", "z", "y", "x")
COLS = ("z", "y", "x")
LANES = 128
TAIL = 8
F32 = jnp.float32
BF16 = jnp.bfloat16
ACROSS = (((1,), (1,)), ((), ()))
DOWN = (((1,), (0,)), ((), ()))
WHOLE = pl.BlockSpec(memory_space=pltpu.VMEM)


def place(core, at):
    turned = [(p + core + s) & (SIDE - 1) for p, s in zip(at, SHIFT)]
    half = [((t + 1) >> 1) & 1 for t in turned]
    pair = [t >> 1 for t in turned]
    return half[0] * 4 + half[1] * 2 + half[2], pair[0] * 4 + pair[1] * 2 + pair[2]


def cube_groups():
    first, second = {}, {}
    for device in range(2 * SIDE**3):
        core, z, y, x = device // 64, device // 16 % 4, device // 4 % 4, device % 4
        half, pair = place(core, (z, y, x))
        first.setdefault((core, pair), {})[half] = device
        second.setdefault((core, half), {})[pair] = device
    in_order = lambda groups: [[group[k] for k in range(CUBE)] for _, group in sorted(groups.items())]
    return in_order(first), in_order(second)


FIRST, SECOND = cube_groups()


def exchange(x, groups):
    return lax.all_to_all(x, AXES, split_axis=0, concat_axis=0, axis_index_groups=groups, tiled=True)


def own_block():
    return place(lax.axis_index("rows"), [lax.axis_index(a) for a in COLS])


def call(kernel, out_shape, name, mib, **kw):
    return pl.pallas_call(
        kernel,
        out_shape=out_shape,
        name=name,
        compiler_params=pltpu.CompilerParams(vmem_limit_bytes=mib << 20),
        **kw,
    )


def array(*shape, dtype=F32):
    return jax.ShapeDtypeStruct(shape, dtype)


def halves(x):
    high = x.astype(BF16)
    return high, (x - high.astype(F32)).astype(BF16)


def dot(a, b, dims):
    return lax.dot_general(a, b, dims, preferred_element_type=F32)


def diagonal(samples):
    shape = (samples, LANES)
    return lax.broadcasted_iota(jnp.int32, shape, 0) == lax.broadcasted_iota(jnp.int32, shape, 1)


def to_lanes(column):
    samples = column.shape[0]
    row = jnp.sum(jnp.where(diagonal(samples), column, 0.0), axis=0, keepdims=True)
    return jnp.broadcast_to(row, (TAIL, LANES))


def to_column(row, samples):
    return jnp.sum(jnp.where(diagonal(samples), row, 0.0), axis=1, keepdims=True)


def stacked(x):
    high, low = halves(x)
    return jnp.concatenate([high, low], 0), high


def put_parts(out_ref, both, high, jac_high_ref, jac_low_ref, tail):
    samples = high.shape[0]
    rows = jac_high_ref.shape[0]
    part = rows // CUBE
    tiles = part // LANES
    for j in range(CUBE):
        at = slice(j * part, (j + 1) * part)
        wide = dot(both, jac_high_ref[at], ACROSS)
        logits = wide[:samples] + wide[samples:] + dot(high, jac_low_ref[at], ACROSS)
        for t in range(tiles):
            out_ref[j, t * samples : (t + 1) * samples] = logits[:, t * LANES : (t + 1) * LANES]
        out_ref[j, tiles * samples :] = tail


def open_kernel(at_ref, theta_ref, targets_ref, jac_ref, out_ref, own_ref, high_ref, low_ref, both_ref):
    samples, cols = theta_ref.shape[1:]
    member = pl.program_id(0)
    lanes = pl.ds(pl.multiple_of(member * cols, cols), cols)
    jac_high, jac_low = halves(jac_ref[0])
    high_ref[:, lanes] = jac_high
    low_ref[:, lanes] = jac_low
    both_ref[:, lanes], _ = stacked(theta_ref[0])

    @pl.when(member == CUBE - 1)
    def _():
        for t in range(targets_ref.shape[1] // LANES):
            own_ref[t * samples : (t + 1) * samples] = targets_ref[:, t * LANES : (t + 1) * LANES]
        both = both_ref[...]
        put_parts(out_ref, both, both[:samples], high_ref, low_ref, jnp.zeros((TAIL, LANES), F32))


def opened(at, theta, targets, jacobian):
    samples, cols = theta.shape[1:]
    rows = jacobian.shape[1]
    block = rows // CUBE
    length = block // LANES * samples
    return pl.pallas_call(
        open_kernel,
        name="opened",
        out_shape=[
            array(CUBE, length + TAIL, LANES),
            array(length, LANES),
            array(rows, CUBE * cols, dtype=BF16),
            array(rows, CUBE * cols, dtype=BF16),
        ],
        grid_spec=pltpu.PrefetchScalarGridSpec(
            num_scalar_prefetch=1,
            grid=(CUBE,),
            in_specs=[
                pl.BlockSpec((1, samples, cols), lambda i, at: (i, 0, 0)),
                pl.BlockSpec((samples, block), lambda i, at: (0, at[0])),
                pl.BlockSpec((1, rows, cols), lambda i, at: (i, 0, 0)),
            ],
            out_specs=[WHOLE] * 4,
            scratch_shapes=[pltpu.VMEM((2 * samples, CUBE * cols), BF16)],
        ),
        compiler_params=pltpu.CompilerParams(vmem_limit_bytes=16 << 20),
    )(at, theta, in_hbm(targets), in_hbm(jacobian))


def in_hbm(x):
    return pltpu.with_memory_space_constraint(x, pltpu.HBM)


def fold_kernel(in_ref, out_ref):
    out_ref[...] = jnp.sum(in_ref[...], axis=0)


def fold(parts):
    return call(fold_kernel, array(*parts.shape[1:]), "fold", 4, in_specs=[WHOLE], out_specs=WHOLE)(parts)


def scale_from(row, samples, clip_level, params):
    squares = to_column(row, samples)
    return jnp.minimum(1.0, clip_level / jnp.sqrt(squares / params + 1e-06))


def residual_to(out_ref, logits, targets):
    residual = jax.nn.sigmoid(logits) - targets
    for i in range(CUBE):
        out_ref[i] = residual


def first_residual_kernel(in_ref, targets_ref, residual_ref, logits_ref):
    logits = jnp.sum(in_ref[:, : targets_ref.shape[0]], axis=0)
    logits_ref[...] = logits
    residual_to(residual_ref, logits, targets_ref[...])


def first_residual(parts, targets):
    return call(
        first_residual_kernel,
        [array(CUBE, *targets.shape), array(*targets.shape)],
        "first_residual",
        4,
        in_specs=[WHOLE] * 2,
        out_specs=[WHOLE] * 2,
    )(parts, targets)


def next_residual(parts, targets, logits, slope, samples, clip_level, params):
    def kernel(in_ref, targets_ref, logits_ref, slope_ref, residual_ref, out_logits_ref, out_slope_ref, scale_ref):
        length = targets_ref.shape[0]
        row = jnp.sum(in_ref[:, length:], axis=0)[:1]
        scale = scale_from(row, samples, clip_level, params)
        scale_ref[...] = jnp.broadcast_to(scale, scale_ref.shape)
        moved = jnp.sum(in_ref[:, :length], axis=0)
        for t in range(length // samples):
            at = slice(t * samples, (t + 1) * samples)
            out_slope_ref[at] = 0.9 * slope_ref[at] + scale * moved[at]
        logits = logits_ref[...] - 0.5 * out_slope_ref[...]
        out_logits_ref[...] = logits
        residual_to(residual_ref, logits, targets_ref[...])

    shape = targets.shape
    return call(
        kernel,
        [array(CUBE, *shape), array(*shape), array(*shape), array(samples, LANES)],
        "next_residual",
        4,
        in_specs=[WHOLE] * 4,
        out_specs=[WHOLE] * 4,
    )(parts, targets, logits, slope)


def joined(in_ref, samples):
    blocks, length = in_ref.shape[0], in_ref.shape[1] // samples * samples
    return jnp.concatenate([in_ref[b, t : t + samples] for b in range(blocks) for t in range(0, length, samples)], 1)


def gradient_kernel(residual_ref, high_ref, low_ref, out_ref):
    samples, cols = out_ref.shape[1:]
    both, high = stacked(joined(residual_ref, samples))
    for c in range(CUBE):
        at = slice(c * cols, (c + 1) * cols)
        wide = dot(both, high_ref[:, at], DOWN)
        out_ref[c] = wide[:samples] + wide[samples:] + dot(high, low_ref[:, at], DOWN)


def gradient_parts(residual, high, low, samples):
    return call(
        gradient_kernel,
        array(CUBE, samples, high.shape[1] // CUBE),
        "gradient",
        16,
        in_specs=[WHOLE] * 3,
        out_specs=WHOLE,
    )(residual, high, low)


def moved_on(state):
    theta_ref, velocity_ref, gradient_ref, scale_ref = state
    velocity = 0.9 * velocity_ref[...] + scale_ref[:, :1] * gradient_ref[...]
    return theta_ref[...] - 0.5 * velocity, velocity


def whole_gradient(own_ref, other_ref, prec_ref, anchor_ref, theta):
    gradient = own_ref[...] + other_ref[...] + prec_ref[...] * (theta - anchor_ref[...])
    return gradient, jnp.sum(gradient * gradient, axis=1, keepdims=True)


def send_gradient(out_ref, gradient, square):
    samples, cols = gradient.shape
    tail = to_lanes(square)
    for c in range(CUBE):
        for t in range(cols // LANES):
            out_ref[c, t * samples : (t + 1) * samples] = gradient[:, t * LANES : (t + 1) * LANES]
        out_ref[c, cols // LANES * samples :] = tail


def first_step_kernel(own_ref, other_ref, prec_ref, anchor_ref, out_ref, gradient_ref):
    gradient, square = whole_gradient(own_ref, other_ref, prec_ref, anchor_ref, anchor_ref[...])
    gradient_ref[...] = gradient
    send_gradient(out_ref, gradient, square)


def next_step_kernel(own_ref, other_ref, prec_ref, anchor_ref, *refs):
    state, (out_ref, gradient_ref, theta_ref, velocity_ref) = refs[:4], refs[4:]
    theta, velocity = moved_on(state)
    theta_ref[...] = theta
    velocity_ref[...] = velocity
    gradient, square = whole_gradient(own_ref, other_ref, prec_ref, anchor_ref, theta)
    gradient_ref[...] = gradient
    send_gradient(out_ref, gradient, square)


def stepped(own, other, prec, anchor, state=()):
    samples, cols = anchor.shape
    outs = 3 if state else 1
    return call(
        next_step_kernel if state else first_step_kernel,
        [array(CUBE, cols // LANES * samples + TAIL, LANES)] + [array(samples, cols)] * outs,
        "next_step" if state else "first_step",
        4,
        in_specs=[WHOLE] * (4 + len(state)),
        out_specs=[WHOLE] * (1 + outs),
    )(own, other, prec, anchor, *state)


def push(parts, high, low, samples):
    def kernel(in_ref, high_ref, low_ref, out_ref):
        both, first = stacked(joined(in_ref, samples))
        tail = jnp.sum(in_ref[:, -TAIL:], axis=0)
        put_parts(out_ref, both, first, high_ref, low_ref, tail)

    rows = high.shape[0]
    return call(
        kernel,
        array(CUBE, rows // CUBE // LANES * samples + TAIL, LANES),
        "push",
        16,
        in_specs=[WHOLE] * 3,
        out_specs=WHOLE,
    )(parts, high, low)


def last_kernel(own_ref, other_ref, prec_ref, anchor_ref, *refs):
    state, (squares_ref, gradient_ref, theta_ref, velocity_ref) = refs[:4], refs[4:]
    theta, velocity = moved_on(state)
    theta_ref[...] = theta
    velocity_ref[...] = velocity
    gradient, square = whole_gradient(own_ref, other_ref, prec_ref, anchor_ref, theta)
    gradient_ref[...] = gradient
    squares_ref[...] = jnp.broadcast_to(to_lanes(square)[:1], squares_ref.shape)


def last_gradient(own, other, prec, anchor, state):
    shape = anchor.shape
    return call(
        last_kernel,
        [array(SIDE**3, LANES)] + [array(*shape)] * 3,
        "last_gradient",
        4,
        in_specs=[WHOLE] * 8,
        out_specs=[WHOLE] * 4,
    )(own, other, prec, anchor, *state)


def close(squares, theta, velocity, gradient, clip_level, params):
    samples = theta.shape[0]

    def kernel(squares_ref, theta_ref, velocity_ref, gradient_ref, out_ref):
        row = jnp.sum(squares_ref[...], axis=0, keepdims=True)
        scale = scale_from(row, samples, clip_level, params)
        velocity = 0.9 * velocity_ref[...] + scale * gradient_ref[...]
        out_ref[...] = theta_ref[...] - 0.5 * velocity

    return call(kernel, array(*theta.shape), "close", 4, in_specs=[WHOLE] * 4, out_specs=WHOLE)(
        squares, theta, velocity, gradient
    )


def body(jacobian, targets, anchor, precision):
    samples, col_dev = anchor.shape
    row_dev = jacobian.shape[0]
    params = col_dev * SIDE**3
    clip_level = 0.2 * math.sqrt(row_dev * 2 / params)
    half, pair = own_block()
    at = jnp.reshape(pair * CUBE + half, (1,)).astype(jnp.int32)
    prec = precision[None, :]
    theta = exchange(jnp.broadcast_to(anchor[None], (CUBE, samples, col_dev)), SECOND)
    square = exchange(jacobian.reshape(CUBE, row_dev // CUBE, col_dev), SECOND)
    parts, own, high, low = opened(at, theta, targets, square)
    residual, logits = first_residual(exchange(parts, FIRST), own)
    slope = jnp.zeros_like(logits)
    state = ()
    for step in range(STEPS):
        parts = gradient_parts(exchange(residual, FIRST), high, low, samples)
        gradient = fold(exchange(parts, SECOND))
        other = lax.ppermute(gradient, "rows", [(0, 1), (1, 0)])
        if step + 1 == STEPS:
            break
        parts, gradient, *moved = stepped(gradient, other, prec, anchor, state)
        theta, velocity = moved if moved else (anchor, jnp.zeros_like(anchor))
        parts = exchange(push(exchange(parts, SECOND), high, low, samples), FIRST)
        residual, logits, slope, scale = next_residual(parts, own, logits, slope, samples, clip_level, params)
        state = (theta, velocity, gradient, scale)
    squares, gradient, theta, velocity = last_gradient(gradient, other, prec, anchor, state)
    squares = lax.all_to_all(squares, COLS, split_axis=0, concat_axis=0, tiled=True)
    return close(squares, theta, velocity, gradient, clip_level, params)


def solution(mesh):
    cubes = Mesh(mesh.devices.reshape(2, SIDE, SIDE, SIDE), AXES)
    in_specs = (P("rows", COLS), P(None, "rows"), P(None, COLS), P(COLS))
    out_specs = P(None, COLS)
    return jax.shard_map(body, mesh=cubes, in_specs=in_specs, out_specs=out_specs, check_vma=False)
```

```python
import math

import jax
import jax.numpy as jnp
from jax import lax
from jax.experimental import pallas as pl
from jax.experimental.pallas import tpu as pltpu
from jax.sharding import Mesh
from jax.sharding import PartitionSpec as P

STEPS = 3
SIDE = 4
CUBE = 8
SHIFT = (0, 1, 1)
AXES = ("rows", "z", "y", "x")
COLS = ("z", "y", "x")
LANES = 128
TAIL = 8
F32 = jnp.float32
BF16 = jnp.bfloat16
ACROSS = (((1,), (1,)), ((), ()))
DOWN = (((1,), (0,)), ((), ()))
WHOLE = pl.BlockSpec(memory_space=pltpu.VMEM)


def place(core, at):
    turned = [(p + core + s) & (SIDE - 1) for p, s in zip(at, SHIFT)]
    half = [((t + 1) >> 1) & 1 for t in turned]
    pair = [t >> 1 for t in turned]
    return half[0] * 4 + half[1] * 2 + half[2], pair[0] * 4 + pair[1] * 2 + pair[2]


def cube_groups():
    first, second = {}, {}
    for device in range(2 * SIDE**3):
        core, z, y, x = device // 64, device // 16 % 4, device // 4 % 4, device % 4
        half, pair = place(core, (z, y, x))
        first.setdefault((core, pair), {})[half] = device
        second.setdefault((core, half), {})[pair] = device
    in_order = lambda groups: [[group[k] for k in range(CUBE)] for _, group in sorted(groups.items())]
    return in_order(first), in_order(second)


FIRST, SECOND = cube_groups()


def at_distance(m):
    return [(group[k], group[k ^ m]) for group in SECOND for k in range(CUBE)]


def exchange(x, groups):
    return lax.all_to_all(x, AXES, split_axis=0, concat_axis=0, axis_index_groups=groups, tiled=True)


def own_block():
    return place(lax.axis_index("rows"), [lax.axis_index(a) for a in COLS])


def call(kernel, out_shape, name, mib, **kw):
    return pl.pallas_call(
        kernel,
        out_shape=out_shape,
        name=name,
        compiler_params=pltpu.CompilerParams(vmem_limit_bytes=mib << 20),
        **kw,
    )


def array(*shape, dtype=F32):
    return jax.ShapeDtypeStruct(shape, dtype)


def halves(x):
    high = x.astype(BF16)
    return high, (x - high.astype(F32)).astype(BF16)


def dot(a, b, dims):
    return lax.dot_general(a, b, dims, preferred_element_type=F32)


def diagonal(samples):
    shape = (samples, LANES)
    return lax.broadcasted_iota(jnp.int32, shape, 0) == lax.broadcasted_iota(jnp.int32, shape, 1)


def to_lanes(column):
    samples = column.shape[0]
    row = jnp.sum(jnp.where(diagonal(samples), column, 0.0), axis=0, keepdims=True)
    return jnp.broadcast_to(row, (TAIL, LANES))


def to_column(row, samples):
    return jnp.sum(jnp.where(diagonal(samples), row, 0.0), axis=1, keepdims=True)


def stacked(x):
    high, low = halves(x)
    return jnp.concatenate([high, low], 0), high


def put_part(out_ref, j, both, high, jac_high, jac_low, tail):
    samples = high.shape[0]
    tiles = jac_high.shape[0] // LANES
    wide = dot(both, jac_high, ACROSS)
    logits = wide[:samples] + wide[samples:] + dot(high, jac_low, ACROSS)
    for t in range(tiles):
        out_ref[j, t * samples : (t + 1) * samples] = logits[:, t * LANES : (t + 1) * LANES]
    out_ref[j, tiles * samples :] = tail


def own_targets(at, targets, block):
    samples = targets.shape[0]

    def kernel(at_ref, targets_ref, out_ref):
        for t in range(block // LANES):
            out_ref[t * samples : (t + 1) * samples] = targets_ref[:, t * LANES : (t + 1) * LANES]

    return pl.pallas_call(
        kernel,
        name="own_targets",
        out_shape=array(block // LANES * samples, LANES),
        grid_spec=pltpu.PrefetchScalarGridSpec(
            num_scalar_prefetch=1,
            grid=(1,),
            in_specs=[pl.BlockSpec((samples, block), lambda i, at: (0, at[0]))],
            out_specs=WHOLE,
        ),
        compiler_params=pltpu.CompilerParams(vmem_limit_bytes=4 << 20),
    )(at, in_hbm(targets))


def open_kernel(pair_ref, theta_ref, jac_ref, out_ref, high_ref, low_ref, both_ref):
    samples, cols = theta_ref.shape[1:]
    part = jac_ref.shape[1]

    @pl.when(pl.program_id(0) == 0)
    def _():
        for c in range(CUBE):
            both_ref[:, c * cols : (c + 1) * cols], _ = stacked(theta_ref[c ^ pair_ref[0]])

    rows = pl.ds(pl.multiple_of(pl.program_id(0) * part, part), part)
    for c in range(CUBE):
        jac_high, jac_low = halves(jac_ref[c])
        high_ref[rows, c * cols : (c + 1) * cols] = jac_high
        low_ref[rows, c * cols : (c + 1) * cols] = jac_low
    both = both_ref[...]
    put_part(out_ref, 0, both, both[:samples], high_ref[rows], low_ref[rows], jnp.zeros((TAIL, LANES), F32))


def opened(pair, theta, jacobian):
    samples, cols = theta.shape[1:]
    rows = jacobian.shape[1]
    part = rows // CUBE
    length = part // LANES * samples + TAIL
    return pl.pallas_call(
        open_kernel,
        name="opened",
        out_shape=[
            array(CUBE, length, LANES),
            array(rows, CUBE * cols, dtype=BF16),
            array(rows, CUBE * cols, dtype=BF16),
        ],
        grid_spec=pltpu.PrefetchScalarGridSpec(
            num_scalar_prefetch=1,
            grid=(CUBE,),
            in_specs=[WHOLE, pl.BlockSpec((CUBE, part, cols), lambda j, pair: (0, j, 0))],
            out_specs=[pl.BlockSpec((1, length, LANES), lambda j, pair: (j, 0, 0)), WHOLE, WHOLE],
            scratch_shapes=[pltpu.VMEM((2 * samples, CUBE * cols), BF16)],
        ),
        compiler_params=pltpu.CompilerParams(vmem_limit_bytes=16 << 20),
    )(pair, theta, in_hbm(jacobian))


def in_hbm(x):
    return pltpu.with_memory_space_constraint(x, pltpu.HBM)


def fold_kernel(in_ref, out_ref):
    out_ref[...] = jnp.sum(in_ref[...], axis=0)


def fold(parts):
    return call(fold_kernel, array(*parts.shape[1:]), "fold", 4, in_specs=[WHOLE], out_specs=WHOLE)(parts)


def scale_from(row, samples, clip_level, params):
    squares = to_column(row, samples)
    return jnp.minimum(1.0, clip_level / jnp.sqrt(squares / params + 1e-06))


def residual_to(out_ref, logits, targets):
    residual = jax.nn.sigmoid(logits) - targets
    for i in range(CUBE):
        out_ref[i] = residual


def first_residual_kernel(in_ref, targets_ref, residual_ref, logits_ref):
    logits = jnp.sum(in_ref[:, : targets_ref.shape[0]], axis=0)
    logits_ref[...] = logits
    residual_to(residual_ref, logits, targets_ref[...])


def first_residual(parts, targets):
    return call(
        first_residual_kernel,
        [array(CUBE, *targets.shape), array(*targets.shape)],
        "first_residual",
        4,
        in_specs=[WHOLE] * 2,
        out_specs=[WHOLE] * 2,
    )(parts, targets)


def next_residual(parts, targets, logits, slope, samples, clip_level, params):
    def kernel(in_ref, targets_ref, logits_ref, slope_ref, residual_ref, out_logits_ref, out_slope_ref, scale_ref):
        length = targets_ref.shape[0]
        row = jnp.sum(in_ref[:, length:], axis=0)[:1]
        scale = scale_from(row, samples, clip_level, params)
        scale_ref[...] = jnp.broadcast_to(scale, scale_ref.shape)
        moved = jnp.sum(in_ref[:, :length], axis=0)
        for t in range(length // samples):
            at = slice(t * samples, (t + 1) * samples)
            out_slope_ref[at] = 0.9 * slope_ref[at] + scale * moved[at]
        logits = logits_ref[...] - 0.5 * out_slope_ref[...]
        out_logits_ref[...] = logits
        residual_to(residual_ref, logits, targets_ref[...])

    shape = targets.shape
    return call(
        kernel,
        [array(CUBE, *shape), array(*shape), array(*shape), array(samples, LANES)],
        "next_residual",
        4,
        in_specs=[WHOLE] * 4,
        out_specs=[WHOLE] * 4,
    )(parts, targets, logits, slope)


def joined(in_ref, samples):
    blocks, length = in_ref.shape[0], in_ref.shape[1] // samples * samples
    return jnp.concatenate([in_ref[b, t : t + samples] for b in range(blocks) for t in range(0, length, samples)], 1)


def gradient_kernel(residual_ref, high_ref, low_ref, out_ref):
    samples, cols = out_ref.shape[1:]
    both, high = stacked(joined(residual_ref, samples))
    for c in range(CUBE):
        at = slice(c * cols, (c + 1) * cols)
        wide = dot(both, high_ref[:, at], DOWN)
        out_ref[c] = wide[:samples] + wide[samples:] + dot(high, low_ref[:, at], DOWN)


def gradient_parts(residual, high, low, samples):
    return call(
        gradient_kernel,
        array(CUBE, samples, high.shape[1] // CUBE),
        "gradient",
        16,
        in_specs=[WHOLE] * 3,
        out_specs=WHOLE,
    )(residual, high, low)


def moved_on(state):
    theta_ref, velocity_ref, gradient_ref, scale_ref = state
    velocity = 0.9 * velocity_ref[...] + scale_ref[:, :1] * gradient_ref[...]
    return theta_ref[...] - 0.5 * velocity, velocity


def whole_gradient(own_ref, other_ref, prec_ref, anchor_ref, theta):
    gradient = own_ref[...] + other_ref[...] + prec_ref[...] * (theta - anchor_ref[...])
    return gradient, jnp.sum(gradient * gradient, axis=1, keepdims=True)


def send_gradient(out_ref, gradient, square):
    samples, cols = gradient.shape
    tail = to_lanes(square)
    for c in range(CUBE):
        for t in range(cols // LANES):
            out_ref[c, t * samples : (t + 1) * samples] = gradient[:, t * LANES : (t + 1) * LANES]
        out_ref[c, cols // LANES * samples :] = tail


def first_step_kernel(own_ref, other_ref, prec_ref, anchor_ref, out_ref, gradient_ref):
    gradient, square = whole_gradient(own_ref, other_ref, prec_ref, anchor_ref, anchor_ref[...])
    gradient_ref[...] = gradient
    send_gradient(out_ref, gradient, square)


def next_step_kernel(own_ref, other_ref, prec_ref, anchor_ref, *refs):
    state, (out_ref, gradient_ref, theta_ref, velocity_ref) = refs[:4], refs[4:]
    theta, velocity = moved_on(state)
    theta_ref[...] = theta
    velocity_ref[...] = velocity
    gradient, square = whole_gradient(own_ref, other_ref, prec_ref, anchor_ref, theta)
    gradient_ref[...] = gradient
    send_gradient(out_ref, gradient, square)


def stepped(own, other, prec, anchor, state=()):
    samples, cols = anchor.shape
    outs = 3 if state else 1
    return call(
        next_step_kernel if state else first_step_kernel,
        [array(CUBE, cols // LANES * samples + TAIL, LANES)] + [array(samples, cols)] * outs,
        "next_step" if state else "first_step",
        4,
        in_specs=[WHOLE] * (4 + len(state)),
        out_specs=[WHOLE] * (1 + outs),
    )(own, other, prec, anchor, *state)


def push(parts, high, low, samples):
    def kernel(in_ref, high_ref, low_ref, out_ref):
        both, first = stacked(joined(in_ref, samples))
        tail = jnp.sum(in_ref[:, -TAIL:], axis=0)
        part = high_ref.shape[0] // CUBE
        for j in range(CUBE):
            at = slice(j * part, (j + 1) * part)
            put_part(out_ref, j, both, first, high_ref[at], low_ref[at], tail)

    rows = high.shape[0]
    return call(
        kernel,
        array(CUBE, rows // CUBE // LANES * samples + TAIL, LANES),
        "push",
        16,
        in_specs=[WHOLE] * 3,
        out_specs=WHOLE,
    )(parts, high, low)


def last_kernel(own_ref, other_ref, prec_ref, anchor_ref, *refs):
    state, (squares_ref, gradient_ref, theta_ref, velocity_ref) = refs[:4], refs[4:]
    theta, velocity = moved_on(state)
    theta_ref[...] = theta
    velocity_ref[...] = velocity
    gradient, square = whole_gradient(own_ref, other_ref, prec_ref, anchor_ref, theta)
    gradient_ref[...] = gradient
    squares_ref[...] = jnp.broadcast_to(to_lanes(square)[:1], squares_ref.shape)


def last_gradient(own, other, prec, anchor, state):
    shape = anchor.shape
    return call(
        last_kernel,
        [array(SIDE**3, LANES)] + [array(*shape)] * 3,
        "last_gradient",
        4,
        in_specs=[WHOLE] * 8,
        out_specs=[WHOLE] * 4,
    )(own, other, prec, anchor, *state)


def close(squares, theta, velocity, gradient, clip_level, params):
    samples = theta.shape[0]

    def kernel(squares_ref, theta_ref, velocity_ref, gradient_ref, out_ref):
        row = jnp.sum(squares_ref[...], axis=0, keepdims=True)
        scale = scale_from(row, samples, clip_level, params)
        velocity = 0.9 * velocity_ref[...] + scale * gradient_ref[...]
        out_ref[...] = theta_ref[...] - 0.5 * velocity

    return call(kernel, array(*theta.shape), "close", 4, in_specs=[WHOLE] * 4, out_specs=WHOLE)(
        squares, theta, velocity, gradient
    )


def body(jacobian, targets, anchor, precision):
    samples, col_dev = anchor.shape
    row_dev = jacobian.shape[0]
    params = col_dev * SIDE**3
    clip_level = 0.2 * math.sqrt(row_dev * 2 / params)
    half, pair = own_block()
    at = jnp.reshape(pair * CUBE + half, (1,)).astype(jnp.int32)
    prec = precision[None, :]
    square = exchange(jacobian.reshape(CUBE, row_dev // CUBE, col_dev), SECOND)
    own = own_targets(at, targets, row_dev // CUBE**2)
    theta = jnp.stack([anchor] + [lax.ppermute(anchor, AXES, at_distance(m)) for m in range(1, CUBE)])
    square, own = lax.optimization_barrier((square, own))
    parts, high, low = opened(jnp.reshape(pair, (1,)).astype(jnp.int32), theta, square)
    residual, logits = first_residual(exchange(parts, FIRST), own)
    slope = jnp.zeros_like(logits)
    state = ()
    for step in range(STEPS):
        parts = gradient_parts(exchange(residual, FIRST), high, low, samples)
        gradient = fold(exchange(parts, SECOND))
        other = lax.ppermute(gradient, "rows", [(0, 1), (1, 0)])
        if step + 1 == STEPS:
            break
        parts, gradient, *moved = stepped(gradient, other, prec, anchor, state)
        theta, velocity = moved if moved else (anchor, jnp.zeros_like(anchor))
        parts = exchange(push(exchange(parts, SECOND), high, low, samples), FIRST)
        residual, logits, slope, scale = next_residual(parts, own, logits, slope, samples, clip_level, params)
        state = (theta, velocity, gradient, scale)
    squares, gradient, theta, velocity = last_gradient(gradient, other, prec, anchor, state)
    squares = lax.all_to_all(squares, COLS, split_axis=0, concat_axis=0, tiled=True)
    return close(squares, theta, velocity, gradient, clip_level, params)


def solution(mesh):
    cubes = Mesh(mesh.devices.reshape(2, SIDE, SIDE, SIDE), AXES)
    in_specs = (P("rows", COLS), P(None, "rows"), P(None, COLS), P(COLS))
    out_specs = P(None, COLS)
    return jax.shard_map(body, mesh=cubes, in_specs=in_specs, out_specs=out_specs, check_vma=False)
```

```python
import math

import jax
import jax.numpy as jnp
from jax import lax
from jax.experimental import pallas as pl
from jax.experimental.pallas import tpu as pltpu
from jax.sharding import Mesh
from jax.sharding import PartitionSpec as P

STEPS = 3
SIDE = 4
CUBE = 8
SHIFT = (0, 1, 1)
AXES = ("rows", "z", "y", "x")
COLS = ("z", "y", "x")
LANES = 128
TAIL = 8
F32 = jnp.float32
BF16 = jnp.bfloat16
ACROSS = (((1,), (1,)), ((), ()))
DOWN = (((1,), (0,)), ((), ()))
WHOLE = pl.BlockSpec(memory_space=pltpu.VMEM)


def place(core, at):
    turned = [(p + core + s) & (SIDE - 1) for p, s in zip(at, SHIFT)]
    half = [((t + 1) >> 1) & 1 for t in turned]
    pair = [t >> 1 for t in turned]
    return half[0] * 4 + half[1] * 2 + half[2], pair[0] * 4 + pair[1] * 2 + pair[2]


def cube_groups():
    first, second = {}, {}
    for device in range(2 * SIDE**3):
        core, z, y, x = device // 64, device // 16 % 4, device // 4 % 4, device % 4
        half, pair = place(core, (z, y, x))
        first.setdefault((core, pair), {})[half] = device
        second.setdefault((core, half), {})[pair] = device
    in_order = lambda groups: [[group[k] for k in range(CUBE)] for _, group in sorted(groups.items())]
    return in_order(first), in_order(second)


FIRST, SECOND = cube_groups()


def at_distance(m):
    return [(group[k], group[k ^ m]) for group in SECOND for k in range(CUBE)]


def exchange(x, groups):
    return lax.all_to_all(x, AXES, split_axis=0, concat_axis=0, axis_index_groups=groups, tiled=True)


def own_block():
    return place(lax.axis_index("rows"), [lax.axis_index(a) for a in COLS])


def call(kernel, out_shape, name, mib, **kw):
    return pl.pallas_call(
        kernel,
        out_shape=out_shape,
        name=name,
        compiler_params=pltpu.CompilerParams(vmem_limit_bytes=mib << 20),
        **kw,
    )


def array(*shape, dtype=F32):
    return jax.ShapeDtypeStruct(shape, dtype)


def halves(x):
    high = x.astype(BF16)
    return high, (x - high.astype(F32)).astype(BF16)


def dot(a, b, dims):
    return lax.dot_general(a, b, dims, preferred_element_type=F32)


def diagonal(samples):
    shape = (samples, LANES)
    return lax.broadcasted_iota(jnp.int32, shape, 0) == lax.broadcasted_iota(jnp.int32, shape, 1)


def to_lanes(column):
    samples = column.shape[0]
    row = jnp.sum(jnp.where(diagonal(samples), column, 0.0), axis=0, keepdims=True)
    return jnp.broadcast_to(row, (TAIL, LANES))


def to_column(row, samples):
    return jnp.sum(jnp.where(diagonal(samples), row, 0.0), axis=1, keepdims=True)


def stacked(x):
    high, low = halves(x)
    return jnp.concatenate([high, low], 0), high


def put_part(out_ref, j, both, high, flip_high, flip_low, tail):
    samples = high.shape[0]
    tiles = flip_high.shape[1] // LANES
    wide = dot(both, flip_high, DOWN)
    logits = wide[:samples] + wide[samples:] + dot(high, flip_low, DOWN)
    for t in range(tiles):
        out_ref[j, t * samples : (t + 1) * samples] = logits[:, t * LANES : (t + 1) * LANES]
    out_ref[j, tiles * samples :] = tail


def own_targets(at, targets, block):
    samples = targets.shape[0]

    def kernel(at_ref, targets_ref, out_ref):
        for t in range(block // LANES):
            out_ref[t * samples : (t + 1) * samples] = targets_ref[:, t * LANES : (t + 1) * LANES]

    return pl.pallas_call(
        kernel,
        name="own_targets",
        out_shape=array(block // LANES * samples, LANES),
        grid_spec=pltpu.PrefetchScalarGridSpec(
            num_scalar_prefetch=1,
            grid=(1,),
            in_specs=[pl.BlockSpec((samples, block), lambda i, at: (0, at[0]))],
            out_specs=WHOLE,
        ),
        compiler_params=pltpu.CompilerParams(vmem_limit_bytes=4 << 20),
    )(at, in_hbm(targets))


def open_kernel(pair_ref, theta_ref, jac_ref, out_ref, high_ref, low_ref, flip_high_ref, flip_low_ref, both_ref):
    samples, cols = theta_ref.shape[1:]
    part = jac_ref.shape[1]

    @pl.when(pl.program_id(0) == 0)
    def _():
        for c in range(CUBE):
            both_ref[:, c * cols : (c + 1) * cols], _ = stacked(theta_ref[c ^ pair_ref[0]])

    rows = pl.ds(pl.multiple_of(pl.program_id(0) * part, part), part)
    for c in range(CUBE):
        jac_high, jac_low = halves(jac_ref[c])
        at = slice(c * cols, (c + 1) * cols)
        high_ref[rows, at] = jac_high
        low_ref[rows, at] = jac_low
        flip_high_ref[pl.program_id(0), at] = jnp.transpose(jac_high)
        flip_low_ref[pl.program_id(0), at] = jnp.transpose(jac_low)
    both = both_ref[...]
    flips = flip_high_ref[pl.program_id(0)], flip_low_ref[pl.program_id(0)]
    put_part(out_ref, 0, both, both[:samples], *flips, jnp.zeros((TAIL, LANES), F32))


def opened(pair, theta, jacobian):
    samples, cols = theta.shape[1:]
    rows = jacobian.shape[1]
    part = rows // CUBE
    length = part // LANES * samples + TAIL
    return pl.pallas_call(
        open_kernel,
        name="opened",
        out_shape=[
            array(CUBE, length, LANES),
            array(rows, CUBE * cols, dtype=BF16),
            array(rows, CUBE * cols, dtype=BF16),
            array(CUBE, CUBE * cols, part, dtype=BF16),
            array(CUBE, CUBE * cols, part, dtype=BF16),
        ],
        grid_spec=pltpu.PrefetchScalarGridSpec(
            num_scalar_prefetch=1,
            grid=(CUBE,),
            in_specs=[WHOLE, pl.BlockSpec((CUBE, part, cols), lambda j, pair: (0, j, 0))],
            out_specs=[pl.BlockSpec((1, length, LANES), lambda j, pair: (j, 0, 0))] + [WHOLE] * 4,
            scratch_shapes=[pltpu.VMEM((2 * samples, CUBE * cols), BF16)],
        ),
        compiler_params=pltpu.CompilerParams(vmem_limit_bytes=12 << 20),
    )(pair, theta, in_hbm(jacobian))


def in_hbm(x):
    return pltpu.with_memory_space_constraint(x, pltpu.HBM)


def fold_kernel(in_ref, out_ref):
    out_ref[...] = jnp.sum(in_ref[...], axis=0)


def fold(parts):
    return call(fold_kernel, array(*parts.shape[1:]), "fold", 4, in_specs=[WHOLE], out_specs=WHOLE)(parts)


def scale_from(row, samples, clip_level, params):
    squares = to_column(row, samples)
    return jnp.minimum(1.0, clip_level / jnp.sqrt(squares / params + 1e-06))


def residual_to(out_ref, logits, targets):
    residual = jax.nn.sigmoid(logits) - targets
    for i in range(CUBE):
        out_ref[i] = residual


def first_residual_kernel(in_ref, targets_ref, residual_ref, logits_ref):
    logits = jnp.sum(in_ref[:, : targets_ref.shape[0]], axis=0)
    logits_ref[...] = logits
    residual_to(residual_ref, logits, targets_ref[...])


def first_residual(parts, targets):
    return call(
        first_residual_kernel,
        [array(CUBE, *targets.shape), array(*targets.shape)],
        "first_residual",
        4,
        in_specs=[WHOLE] * 2,
        out_specs=[WHOLE] * 2,
    )(parts, targets)


def next_residual(parts, targets, logits, slope, samples, clip_level, params):
    def kernel(in_ref, targets_ref, logits_ref, slope_ref, residual_ref, out_logits_ref, out_slope_ref, scale_ref):
        length = targets_ref.shape[0]
        row = jnp.sum(in_ref[:, length:], axis=0)[:1]
        scale = scale_from(row, samples, clip_level, params)
        scale_ref[...] = jnp.broadcast_to(scale, scale_ref.shape)
        moved = jnp.sum(in_ref[:, :length], axis=0)
        for t in range(length // samples):
            at = slice(t * samples, (t + 1) * samples)
            out_slope_ref[at] = 0.9 * slope_ref[at] + scale * moved[at]
        logits = logits_ref[...] - 0.5 * out_slope_ref[...]
        out_logits_ref[...] = logits
        residual_to(residual_ref, logits, targets_ref[...])

    shape = targets.shape
    return call(
        kernel,
        [array(CUBE, *shape), array(*shape), array(*shape), array(samples, LANES)],
        "next_residual",
        4,
        in_specs=[WHOLE] * 4,
        out_specs=[WHOLE] * 4,
    )(parts, targets, logits, slope)


def joined(in_ref, samples):
    blocks, length = in_ref.shape[0], in_ref.shape[1] // samples * samples
    return jnp.concatenate([in_ref[b, t : t + samples] for b in range(blocks) for t in range(0, length, samples)], 1)


def gradient_kernel(residual_ref, high_ref, low_ref, out_ref):
    samples, cols = out_ref.shape[1:]
    both, high = stacked(joined(residual_ref, samples))
    for c in range(CUBE):
        at = slice(c * cols, (c + 1) * cols)
        wide = dot(both, high_ref[:, at], DOWN)
        out_ref[c] = wide[:samples] + wide[samples:] + dot(high, low_ref[:, at], DOWN)


def gradient_parts(residual, high, low, samples):
    return call(
        gradient_kernel,
        array(CUBE, samples, high.shape[1] // CUBE),
        "gradient",
        6,
        in_specs=[WHOLE] * 3,
        out_specs=WHOLE,
    )(residual, high, low)


def moved_on(state):
    theta_ref, velocity_ref, gradient_ref, scale_ref = state
    velocity = 0.9 * velocity_ref[...] + scale_ref[:, :1] * gradient_ref[...]
    return theta_ref[...] - 0.5 * velocity, velocity


def whole_gradient(own_ref, other_ref, prec_ref, anchor_ref, theta):
    gradient = own_ref[...] + other_ref[...] + prec_ref[...] * (theta - anchor_ref[...])
    return gradient, jnp.sum(gradient * gradient, axis=1, keepdims=True)


def send_gradient(out_ref, gradient, square):
    samples, cols = gradient.shape
    tail = to_lanes(square)
    for c in range(CUBE):
        for t in range(cols // LANES):
            out_ref[c, t * samples : (t + 1) * samples] = gradient[:, t * LANES : (t + 1) * LANES]
        out_ref[c, cols // LANES * samples :] = tail


def first_step_kernel(own_ref, other_ref, prec_ref, anchor_ref, out_ref, gradient_ref):
    gradient, square = whole_gradient(own_ref, other_ref, prec_ref, anchor_ref, anchor_ref[...])
    gradient_ref[...] = gradient
    send_gradient(out_ref, gradient, square)


def next_step_kernel(own_ref, other_ref, prec_ref, anchor_ref, *refs):
    state, (out_ref, gradient_ref, theta_ref, velocity_ref) = refs[:4], refs[4:]
    theta, velocity = moved_on(state)
    theta_ref[...] = theta
    velocity_ref[...] = velocity
    gradient, square = whole_gradient(own_ref, other_ref, prec_ref, anchor_ref, theta)
    gradient_ref[...] = gradient
    send_gradient(out_ref, gradient, square)


def stepped(own, other, prec, anchor, state=()):
    samples, cols = anchor.shape
    outs = 3 if state else 1
    return call(
        next_step_kernel if state else first_step_kernel,
        [array(CUBE, cols // LANES * samples + TAIL, LANES)] + [array(samples, cols)] * outs,
        "next_step" if state else "first_step",
        4,
        in_specs=[WHOLE] * (4 + len(state)),
        out_specs=[WHOLE] * (1 + outs),
    )(own, other, prec, anchor, *state)


def push(parts, flip_high, flip_low, samples):
    def kernel(in_ref, high_ref, low_ref, out_ref):
        both, first = stacked(joined(in_ref, samples))
        tail = jnp.sum(in_ref[:, -TAIL:], axis=0)
        for j in range(CUBE):
            put_part(out_ref, j, both, first, high_ref[j], low_ref[j], tail)

    return call(
        kernel,
        array(CUBE, flip_high.shape[2] // LANES * samples + TAIL, LANES),
        "push",
        6,
        in_specs=[WHOLE] * 3,
        out_specs=WHOLE,
    )(parts, flip_high, flip_low)


def last_kernel(own_ref, other_ref, prec_ref, anchor_ref, *refs):
    state, (squares_ref, gradient_ref, theta_ref, velocity_ref) = refs[:4], refs[4:]
    theta, velocity = moved_on(state)
    theta_ref[...] = theta
    velocity_ref[...] = velocity
    gradient, square = whole_gradient(own_ref, other_ref, prec_ref, anchor_ref, theta)
    gradient_ref[...] = gradient
    squares_ref[...] = jnp.broadcast_to(to_lanes(square)[:1], squares_ref.shape)


def last_gradient(own, other, prec, anchor, state):
    shape = anchor.shape
    return call(
        last_kernel,
        [array(SIDE**3, LANES)] + [array(*shape)] * 3,
        "last_gradient",
        4,
        in_specs=[WHOLE] * 8,
        out_specs=[WHOLE] * 4,
    )(own, other, prec, anchor, *state)


def close(squares, theta, velocity, gradient, clip_level, params):
    samples = theta.shape[0]

    def kernel(squares_ref, theta_ref, velocity_ref, gradient_ref, out_ref):
        row = jnp.sum(squares_ref[...], axis=0, keepdims=True)
        scale = scale_from(row, samples, clip_level, params)
        velocity = 0.9 * velocity_ref[...] + scale * gradient_ref[...]
        out_ref[...] = theta_ref[...] - 0.5 * velocity

    return call(kernel, array(*theta.shape), "close", 4, in_specs=[WHOLE] * 4, out_specs=WHOLE)(
        squares, theta, velocity, gradient
    )


def body(jacobian, targets, anchor, precision):
    samples, col_dev = anchor.shape
    row_dev = jacobian.shape[0]
    params = col_dev * SIDE**3
    clip_level = 0.2 * math.sqrt(row_dev * 2 / params)
    half, pair = own_block()
    at = jnp.reshape(pair * CUBE + half, (1,)).astype(jnp.int32)
    prec = precision[None, :]
    square = exchange(jacobian.reshape(CUBE, row_dev // CUBE, col_dev), SECOND)
    own = own_targets(at, targets, row_dev // CUBE**2)
    theta = jnp.stack([anchor] + [lax.ppermute(anchor, AXES, at_distance(m)) for m in range(1, CUBE)])
    square, own = lax.optimization_barrier((square, own))
    parts, high, low, *flips = opened(jnp.reshape(pair, (1,)).astype(jnp.int32), theta, square)
    residual, logits = first_residual(exchange(parts, FIRST), own)
    slope = jnp.zeros_like(logits)
    state = ()
    for step in range(STEPS):
        parts = gradient_parts(exchange(residual, FIRST), high, low, samples)
        gradient = fold(exchange(parts, SECOND))
        other = lax.ppermute(gradient, "rows", [(0, 1), (1, 0)])
        if step + 1 == STEPS:
            break
        parts, gradient, *moved = stepped(gradient, other, prec, anchor, state)
        theta, velocity = moved if moved else (anchor, jnp.zeros_like(anchor))
        parts = exchange(push(exchange(parts, SECOND), *flips, samples), FIRST)
        residual, logits, slope, scale = next_residual(parts, own, logits, slope, samples, clip_level, params)
        state = (theta, velocity, gradient, scale)
    squares, gradient, theta, velocity = last_gradient(gradient, other, prec, anchor, state)
    squares = lax.all_to_all(squares, COLS, split_axis=0, concat_axis=0, tiled=True)
    return close(squares, theta, velocity, gradient, clip_level, params)


def solution(mesh):
    cubes = Mesh(mesh.devices.reshape(2, SIDE, SIDE, SIDE), AXES)
    in_specs = (P("rows", COLS), P(None, "rows"), P(None, COLS), P(COLS))
    out_specs = P(None, COLS)
    return jax.shard_map(body, mesh=cubes, in_specs=in_specs, out_specs=out_specs, check_vma=False)
```

```python
import math

import jax
import jax.numpy as jnp
from jax import lax
from jax.experimental import pallas as pl
from jax.experimental.pallas import tpu as pltpu
from jax.sharding import Mesh
from jax.sharding import PartitionSpec as P

STEPS = 3
SIDE = 4
CUBE = 8
SHIFT = (0, 1, 1)
AXES = ("rows", "z", "y", "x")
COLS = ("z", "y", "x")
LANES = 128
TAIL = 8
F32 = jnp.float32
BF16 = jnp.bfloat16
ACROSS = (((1,), (1,)), ((), ()))
DOWN = (((1,), (0,)), ((), ()))
WHOLE = pl.BlockSpec(memory_space=pltpu.VMEM)


def place(core, at):
    turned = [(p + core + s) & (SIDE - 1) for p, s in zip(at, SHIFT)]
    half = [((t + 1) >> 1) & 1 for t in turned]
    pair = [t >> 1 for t in turned]
    return half[0] * 4 + half[1] * 2 + half[2], pair[0] * 4 + pair[1] * 2 + pair[2]


def cube_groups():
    first, second = {}, {}
    for device in range(2 * SIDE**3):
        core, z, y, x = device // 64, device // 16 % 4, device // 4 % 4, device % 4
        half, pair = place(core, (z, y, x))
        first.setdefault((core, pair), {})[half] = device
        second.setdefault((core, half), {})[pair] = device
    in_order = lambda groups: [[group[k] for k in range(CUBE)] for _, group in sorted(groups.items())]
    return in_order(first), in_order(second)


FIRST, SECOND = cube_groups()


def exchange(x, groups):
    return lax.all_to_all(x, AXES, split_axis=0, concat_axis=0, axis_index_groups=groups, tiled=True)


def own_block():
    return place(lax.axis_index("rows"), [lax.axis_index(a) for a in COLS])


def call(kernel, out_shape, name, mib, **kw):
    return pl.pallas_call(
        kernel,
        out_shape=out_shape,
        name=name,
        compiler_params=pltpu.CompilerParams(vmem_limit_bytes=mib << 20),
        **kw,
    )


def array(*shape, dtype=F32):
    return jax.ShapeDtypeStruct(shape, dtype)


def halves(x):
    high = x.astype(BF16)
    return high, (x - high.astype(F32)).astype(BF16)


def dot(a, b, dims):
    return lax.dot_general(a, b, dims, preferred_element_type=F32)


def diagonal(samples):
    shape = (samples, LANES)
    return lax.broadcasted_iota(jnp.int32, shape, 0) == lax.broadcasted_iota(jnp.int32, shape, 1)


def to_lanes(column):
    samples = column.shape[0]
    row = jnp.sum(jnp.where(diagonal(samples), column, 0.0), axis=0, keepdims=True)
    return jnp.broadcast_to(row, (TAIL, LANES))


def to_column(row, samples):
    return jnp.sum(jnp.where(diagonal(samples), row, 0.0), axis=1, keepdims=True)


def stacked(x):
    high, low = halves(x)
    return jnp.concatenate([high, low], 0), high


def put_part(out_ref, j, both, high, flip_high, flip_low, tail):
    samples = high.shape[0]
    tiles = flip_high.shape[1] // LANES
    wide = dot(both, flip_high, DOWN)
    logits = wide[:samples] + wide[samples:] + dot(high, flip_low, DOWN)
    for t in range(tiles):
        out_ref[j, t * samples : (t + 1) * samples] = logits[:, t * LANES : (t + 1) * LANES]
    out_ref[j, tiles * samples :] = tail


def open_kernel(at_ref, targets_ref, theta_ref, jac_ref, out_ref, own_ref, *refs):
    high_ref, low_ref, flip_high_ref, flip_low_ref, both_ref = refs
    samples, cols = theta_ref.shape[1:]
    j = pl.program_id(0)
    part = jac_ref.shape[1]

    @pl.when(j == 0)
    def _():
        for t in range(targets_ref.shape[1] // LANES):
            own_ref[t * samples : (t + 1) * samples] = targets_ref[:, t * LANES : (t + 1) * LANES]
        for c in range(CUBE):
            both_ref[:, c * cols : (c + 1) * cols], _ = stacked(theta_ref[c])

    rows = pl.ds(pl.multiple_of(j * part, part), part)
    for c in range(CUBE):
        jac_high, jac_low = halves(jac_ref[c])
        at = slice(c * cols, (c + 1) * cols)
        high_ref[rows, at] = jac_high
        low_ref[rows, at] = jac_low
        flip_high_ref[j, at] = jnp.transpose(jac_high)
        flip_low_ref[j, at] = jnp.transpose(jac_low)
    both = both_ref[...]
    put_part(out_ref, 0, both, both[:samples], flip_high_ref[j], flip_low_ref[j], jnp.zeros((TAIL, LANES), F32))


def opened(at, targets, theta, jacobian):
    samples, cols = theta.shape[1:]
    rows = jacobian.shape[1]
    part = rows // CUBE
    length = part // LANES * samples
    return pl.pallas_call(
        open_kernel,
        name="opened",
        out_shape=[
            array(CUBE, length + TAIL, LANES),
            array(length, LANES),
            array(rows, CUBE * cols, dtype=BF16),
            array(rows, CUBE * cols, dtype=BF16),
            array(CUBE, CUBE * cols, part, dtype=BF16),
            array(CUBE, CUBE * cols, part, dtype=BF16),
        ],
        grid_spec=pltpu.PrefetchScalarGridSpec(
            num_scalar_prefetch=1,
            grid=(CUBE,),
            in_specs=[
                pl.BlockSpec((samples, part), lambda j, at: (0, at[0])),
                WHOLE,
                pl.BlockSpec((CUBE, part, cols), lambda j, at: (0, j, 0)),
            ],
            out_specs=[pl.BlockSpec((1, length + TAIL, LANES), lambda j, at: (j, 0, 0))] + [WHOLE] * 5,
            scratch_shapes=[pltpu.VMEM((2 * samples, CUBE * cols), BF16)],
        ),
        compiler_params=pltpu.CompilerParams(vmem_limit_bytes=12 << 20),
    )(at, in_hbm(targets), theta, in_hbm(jacobian))


def in_hbm(x):
    return pltpu.with_memory_space_constraint(x, pltpu.HBM)


def fold_kernel(in_ref, out_ref):
    out_ref[...] = jnp.sum(in_ref[...], axis=0)


def fold(parts):
    return call(fold_kernel, array(*parts.shape[1:]), "fold", 4, in_specs=[WHOLE], out_specs=WHOLE)(parts)


def scale_from(row, samples, clip_level, params):
    squares = to_column(row, samples)
    return jnp.minimum(1.0, clip_level / jnp.sqrt(squares / params + 1e-06))


def residual_to(out_ref, logits, targets):
    residual = jax.nn.sigmoid(logits) - targets
    for i in range(CUBE):
        out_ref[i] = residual


def first_residual_kernel(in_ref, targets_ref, residual_ref, logits_ref):
    logits = jnp.sum(in_ref[:, : targets_ref.shape[0]], axis=0)
    logits_ref[...] = logits
    residual_to(residual_ref, logits, targets_ref[...])


def first_residual(parts, targets):
    return call(
        first_residual_kernel,
        [array(CUBE, *targets.shape), array(*targets.shape)],
        "first_residual",
        4,
        in_specs=[WHOLE] * 2,
        out_specs=[WHOLE] * 2,
    )(parts, targets)


def next_residual(parts, targets, logits, slope, samples, clip_level, params):
    def kernel(in_ref, targets_ref, logits_ref, slope_ref, residual_ref, out_logits_ref, out_slope_ref, scale_ref):
        length = targets_ref.shape[0]
        row = jnp.sum(in_ref[:, length:], axis=0)[:1]
        scale = scale_from(row, samples, clip_level, params)
        scale_ref[...] = jnp.broadcast_to(scale, scale_ref.shape)
        moved = jnp.sum(in_ref[:, :length], axis=0)
        for t in range(length // samples):
            at = slice(t * samples, (t + 1) * samples)
            out_slope_ref[at] = 0.9 * slope_ref[at] + scale * moved[at]
        logits = logits_ref[...] - 0.5 * out_slope_ref[...]
        out_logits_ref[...] = logits
        residual_to(residual_ref, logits, targets_ref[...])

    shape = targets.shape
    return call(
        kernel,
        [array(CUBE, *shape), array(*shape), array(*shape), array(samples, LANES)],
        "next_residual",
        4,
        in_specs=[WHOLE] * 4,
        out_specs=[WHOLE] * 4,
    )(parts, targets, logits, slope)


def joined(in_ref, samples):
    blocks, length = in_ref.shape[0], in_ref.shape[1] // samples * samples
    return jnp.concatenate([in_ref[b, t : t + samples] for b in range(blocks) for t in range(0, length, samples)], 1)


def gradient_kernel(residual_ref, high_ref, low_ref, out_ref):
    samples, cols = out_ref.shape[1:]
    both, high = stacked(joined(residual_ref, samples))
    for c in range(CUBE):
        at = slice(c * cols, (c + 1) * cols)
        wide = dot(both, high_ref[:, at], DOWN)
        out_ref[c] = wide[:samples] + wide[samples:] + dot(high, low_ref[:, at], DOWN)


def gradient_parts(residual, high, low, samples):
    return call(
        gradient_kernel,
        array(CUBE, samples, high.shape[1] // CUBE),
        "gradient",
        6,
        in_specs=[WHOLE] * 3,
        out_specs=WHOLE,
    )(residual, high, low)


def moved_on(state):
    theta_ref, velocity_ref, gradient_ref, scale_ref = state
    velocity = 0.9 * velocity_ref[...] + scale_ref[:, :1] * gradient_ref[...]
    return theta_ref[...] - 0.5 * velocity, velocity


def whole_gradient(own_ref, other_ref, prec_ref, anchor_ref, theta):
    gradient = own_ref[...] + other_ref[...] + prec_ref[...] * (theta - anchor_ref[...])
    return gradient, jnp.sum(gradient * gradient, axis=1, keepdims=True)


def send_gradient(out_ref, gradient, square):
    samples, cols = gradient.shape
    tail = to_lanes(square)
    for c in range(CUBE):
        for t in range(cols // LANES):
            out_ref[c, t * samples : (t + 1) * samples] = gradient[:, t * LANES : (t + 1) * LANES]
        out_ref[c, cols // LANES * samples :] = tail


def first_step_kernel(own_ref, other_ref, prec_ref, anchor_ref, out_ref, gradient_ref):
    gradient, square = whole_gradient(own_ref, other_ref, prec_ref, anchor_ref, anchor_ref[...])
    gradient_ref[...] = gradient
    send_gradient(out_ref, gradient, square)


def next_step_kernel(own_ref, other_ref, prec_ref, anchor_ref, *refs):
    state, (out_ref, gradient_ref, theta_ref, velocity_ref) = refs[:4], refs[4:]
    theta, velocity = moved_on(state)
    theta_ref[...] = theta
    velocity_ref[...] = velocity
    gradient, square = whole_gradient(own_ref, other_ref, prec_ref, anchor_ref, theta)
    gradient_ref[...] = gradient
    send_gradient(out_ref, gradient, square)


def stepped(own, other, prec, anchor, state=()):
    samples, cols = anchor.shape
    outs = 3 if state else 1
    return call(
        next_step_kernel if state else first_step_kernel,
        [array(CUBE, cols // LANES * samples + TAIL, LANES)] + [array(samples, cols)] * outs,
        "next_step" if state else "first_step",
        4,
        in_specs=[WHOLE] * (4 + len(state)),
        out_specs=[WHOLE] * (1 + outs),
    )(own, other, prec, anchor, *state)


def push(parts, flip_high, flip_low, samples):
    def kernel(in_ref, high_ref, low_ref, out_ref):
        both, first = stacked(joined(in_ref, samples))
        tail = jnp.sum(in_ref[:, -TAIL:], axis=0)
        for j in range(CUBE):
            put_part(out_ref, j, both, first, high_ref[j], low_ref[j], tail)

    return call(
        kernel,
        array(CUBE, flip_high.shape[2] // LANES * samples + TAIL, LANES),
        "push",
        6,
        in_specs=[WHOLE] * 3,
        out_specs=WHOLE,
    )(parts, flip_high, flip_low)


def last_kernel(own_ref, other_ref, prec_ref, anchor_ref, *refs):
    state, (squares_ref, gradient_ref, theta_ref, velocity_ref) = refs[:4], refs[4:]
    theta, velocity = moved_on(state)
    theta_ref[...] = theta
    velocity_ref[...] = velocity
    gradient, square = whole_gradient(own_ref, other_ref, prec_ref, anchor_ref, theta)
    gradient_ref[...] = gradient
    squares_ref[...] = jnp.broadcast_to(to_lanes(square)[:1], squares_ref.shape)


def last_gradient(own, other, prec, anchor, state):
    shape = anchor.shape
    return call(
        last_kernel,
        [array(SIDE**3, LANES)] + [array(*shape)] * 3,
        "last_gradient",
        4,
        in_specs=[WHOLE] * 8,
        out_specs=[WHOLE] * 4,
    )(own, other, prec, anchor, *state)


def close(squares, theta, velocity, gradient, clip_level, params):
    samples = theta.shape[0]

    def kernel(squares_ref, theta_ref, velocity_ref, gradient_ref, out_ref):
        row = jnp.sum(squares_ref[...], axis=0, keepdims=True)
        scale = scale_from(row, samples, clip_level, params)
        velocity = 0.9 * velocity_ref[...] + scale * gradient_ref[...]
        out_ref[...] = theta_ref[...] - 0.5 * velocity

    return call(kernel, array(*theta.shape), "close", 4, in_specs=[WHOLE] * 4, out_specs=WHOLE)(
        squares, theta, velocity, gradient
    )


def body(jacobian, targets, anchor, precision):
    samples, col_dev = anchor.shape
    row_dev = jacobian.shape[0]
    params = col_dev * SIDE**3
    clip_level = 0.2 * math.sqrt(row_dev * 2 / params)
    half, pair = own_block()
    at = jnp.reshape(pair * CUBE + half, (1,)).astype(jnp.int32)
    prec = precision[None, :]
    jacobian, at = lax.optimization_barrier((jacobian, at))
    square = exchange(jacobian.reshape(CUBE, row_dev // CUBE, col_dev), SECOND)
    square, theta = lax.optimization_barrier((square, anchor))
    theta = exchange(jnp.broadcast_to(theta[None], (CUBE, samples, col_dev)), SECOND)
    parts, own, high, low, *flips = opened(at, targets, theta, square)
    residual, logits = first_residual(exchange(parts, FIRST), own)
    slope = jnp.zeros_like(logits)
    state = ()
    for step in range(STEPS):
        parts = gradient_parts(exchange(residual, FIRST), high, low, samples)
        gradient = fold(exchange(parts, SECOND))
        other = lax.ppermute(gradient, "rows", [(0, 1), (1, 0)])
        if step + 1 == STEPS:
            break
        parts, gradient, *moved = stepped(gradient, other, prec, anchor, state)
        theta, velocity = moved if moved else (anchor, jnp.zeros_like(anchor))
        parts = exchange(push(exchange(parts, SECOND), *flips, samples), FIRST)
        residual, logits, slope, scale = next_residual(parts, own, logits, slope, samples, clip_level, params)
        state = (theta, velocity, gradient, scale)
    squares, gradient, theta, velocity = last_gradient(gradient, other, prec, anchor, state)
    squares = lax.all_to_all(squares, COLS, split_axis=0, concat_axis=0, tiled=True)
    return close(squares, theta, velocity, gradient, clip_level, params)


def solution(mesh):
    cubes = Mesh(mesh.devices.reshape(2, SIDE, SIDE, SIDE), AXES)
    in_specs = (P("rows", COLS), P(None, "rows"), P(None, COLS), P(COLS))
    out_specs = P(None, COLS)
    return jax.shard_map(body, mesh=cubes, in_specs=in_specs, out_specs=out_specs, check_vma=False)
```

```python
import math

import jax
import jax.numpy as jnp
from jax import lax
from jax.experimental import pallas as pl
from jax.experimental.pallas import tpu as pltpu
from jax.sharding import Mesh
from jax.sharding import PartitionSpec as P

STEPS = 3
SIDE = 4
CUBE = 8
SHIFT = (1, 1, 0)
AXES = ("rows", "z", "y", "x")
COLS = ("z", "y", "x")
LANES = 128
TAIL = 8
F32 = jnp.float32
BF16 = jnp.bfloat16
ACROSS = (((1,), (1,)), ((), ()))
DOWN = (((1,), (0,)), ((), ()))
WHOLE = pl.BlockSpec(memory_space=pltpu.VMEM)


def place(core, at):
    turned = [(p + core + s) & (SIDE - 1) for p, s in zip(at, SHIFT)]
    half = [((t + 1) >> 1) & 1 for t in turned]
    pair = [t >> 1 for t in turned]
    return walk(half), walk(pair)


def walk(bits):
    a, b, c = bits
    return a * 4 + (a ^ b) * 2 + (a ^ b ^ c)


def cube_groups():
    first, second = {}, {}
    for device in range(2 * SIDE**3):
        core, z, y, x = device // 64, device // 16 % 4, device // 4 % 4, device % 4
        half, pair = place(core, (z, y, x))
        first.setdefault((core, pair), {})[half] = device
        second.setdefault((core, half), {})[pair] = device
    in_order = lambda groups: [[group[k] for k in range(CUBE)] for _, group in sorted(groups.items())]
    return in_order(first), in_order(second)


FIRST, SECOND = cube_groups()


def exchange(x, groups):
    return lax.all_to_all(x, AXES, split_axis=0, concat_axis=0, axis_index_groups=groups, tiled=True)


def own_block():
    return place(lax.axis_index("rows"), [lax.axis_index(a) for a in COLS])


def call(kernel, out_shape, name, mib, **kw):
    return pl.pallas_call(
        kernel,
        out_shape=out_shape,
        name=name,
        compiler_params=pltpu.CompilerParams(vmem_limit_bytes=mib << 20),
        **kw,
    )


def array(*shape, dtype=F32):
    return jax.ShapeDtypeStruct(shape, dtype)


def halves(x):
    high = x.astype(BF16)
    return high, (x - high.astype(F32)).astype(BF16)


def dot(a, b, dims):
    return lax.dot_general(a, b, dims, preferred_element_type=F32)


def diagonal(samples):
    shape = (samples, LANES)
    return lax.broadcasted_iota(jnp.int32, shape, 0) == lax.broadcasted_iota(jnp.int32, shape, 1)


def to_lanes(column):
    samples = column.shape[0]
    row = jnp.sum(jnp.where(diagonal(samples), column, 0.0), axis=0, keepdims=True)
    return jnp.broadcast_to(row, (TAIL, LANES))


def to_column(row, samples):
    return jnp.sum(jnp.where(diagonal(samples), row, 0.0), axis=1, keepdims=True)


def stacked(x):
    high, low = halves(x)
    return jnp.concatenate([high, low], 0), high


def put_part(out_ref, j, both, high, flip_high, flip_low, tail):
    samples = high.shape[0]
    tiles = flip_high.shape[1] // LANES
    wide = dot(both, flip_high, DOWN)
    logits = wide[:samples] + wide[samples:] + dot(high, flip_low, DOWN)
    for t in range(tiles):
        out_ref[j, t * samples : (t + 1) * samples] = logits[:, t * LANES : (t + 1) * LANES]
    out_ref[j, tiles * samples :] = tail


def open_kernel(at_ref, targets_ref, theta_ref, jac_ref, out_ref, own_ref, *refs):
    high_ref, low_ref, flip_high_ref, flip_low_ref, both_ref = refs
    samples, cols = theta_ref.shape[1:]
    j = pl.program_id(0)
    part = jac_ref.shape[1]

    @pl.when(j == 0)
    def _():
        for t in range(targets_ref.shape[1] // LANES):
            own_ref[t * samples : (t + 1) * samples] = targets_ref[:, t * LANES : (t + 1) * LANES]
        for c in range(CUBE):
            both_ref[:, c * cols : (c + 1) * cols], _ = stacked(theta_ref[c])

    rows = pl.ds(pl.multiple_of(j * part, part), part)
    for c in range(CUBE):
        jac_high, jac_low = halves(jac_ref[c])
        at = slice(c * cols, (c + 1) * cols)
        high_ref[rows, at] = jac_high
        low_ref[rows, at] = jac_low
        flip_high_ref[j, at] = jnp.transpose(jac_high)
        flip_low_ref[j, at] = jnp.transpose(jac_low)
    both = both_ref[...]
    put_part(out_ref, 0, both, both[:samples], flip_high_ref[j], flip_low_ref[j], jnp.zeros((TAIL, LANES), F32))


def opened(at, targets, theta, jacobian):
    samples, cols = theta.shape[1:]
    rows = jacobian.shape[1]
    part = rows // CUBE
    length = part // LANES * samples
    return pl.pallas_call(
        open_kernel,
        name="opened",
        out_shape=[
            array(CUBE, length + TAIL, LANES),
            array(length, LANES),
            array(rows, CUBE * cols, dtype=BF16),
            array(rows, CUBE * cols, dtype=BF16),
            array(CUBE, CUBE * cols, part, dtype=BF16),
            array(CUBE, CUBE * cols, part, dtype=BF16),
        ],
        grid_spec=pltpu.PrefetchScalarGridSpec(
            num_scalar_prefetch=1,
            grid=(CUBE,),
            in_specs=[
                pl.BlockSpec((samples, part), lambda j, at: (0, at[0])),
                WHOLE,
                pl.BlockSpec((CUBE, part, cols), lambda j, at: (0, j, 0)),
            ],
            out_specs=[pl.BlockSpec((1, length + TAIL, LANES), lambda j, at: (j, 0, 0))] + [WHOLE] * 5,
            scratch_shapes=[pltpu.VMEM((2 * samples, CUBE * cols), BF16)],
        ),
        compiler_params=pltpu.CompilerParams(vmem_limit_bytes=12 << 20),
    )(at, in_hbm(targets), theta, in_hbm(jacobian))


def in_hbm(x):
    return pltpu.with_memory_space_constraint(x, pltpu.HBM)


def fold_kernel(in_ref, out_ref):
    out_ref[...] = jnp.sum(in_ref[...], axis=0)


def fold(parts):
    return call(fold_kernel, array(*parts.shape[1:]), "fold", 4, in_specs=[WHOLE], out_specs=WHOLE)(parts)


def scale_from(row, samples, clip_level, params):
    squares = to_column(row, samples)
    return jnp.minimum(1.0, clip_level / jnp.sqrt(squares / params + 1e-06))


def residual_to(out_ref, logits, targets):
    residual = jax.nn.sigmoid(logits) - targets
    for i in range(CUBE):
        out_ref[i] = residual


def first_residual_kernel(in_ref, targets_ref, residual_ref, logits_ref):
    logits = jnp.sum(in_ref[:, : targets_ref.shape[0]], axis=0)
    logits_ref[...] = logits
    residual_to(residual_ref, logits, targets_ref[...])


def first_residual(parts, targets):
    return call(
        first_residual_kernel,
        [array(CUBE, *targets.shape), array(*targets.shape)],
        "first_residual",
        4,
        in_specs=[WHOLE] * 2,
        out_specs=[WHOLE] * 2,
    )(parts, targets)


def next_residual(parts, targets, logits, slope, samples, clip_level, params, last):
    def kernel(in_ref, targets_ref, logits_ref, slope_ref, residual_ref, scale_ref, *kept):
        length = targets_ref.shape[0]
        row = jnp.sum(in_ref[:, length:], axis=0)[:1]
        scale = scale_from(row, samples, clip_level, params)
        scale_ref[...] = jnp.broadcast_to(scale, scale_ref.shape)
        moved = jnp.sum(in_ref[:, :length], axis=0)
        every = jnp.concatenate([scale] * (length // samples), 0)
        slope = 0.9 * slope_ref[...] + every * moved
        logits = logits_ref[...] - 0.5 * slope
        if kept:
            kept[0][...] = logits
            kept[1][...] = slope
        residual_to(residual_ref, logits, targets_ref[...])

    shape = targets.shape
    kept = 0 if last else 2
    return call(
        kernel,
        [array(CUBE, *shape), array(samples, LANES)] + [array(*shape)] * kept,
        "last_residual" if last else "next_residual",
        4,
        in_specs=[WHOLE] * 4,
        out_specs=[WHOLE] * (2 + kept),
    )(parts, targets, logits, slope)


def joined(in_ref, samples):
    blocks, length = in_ref.shape[0], in_ref.shape[1] // samples * samples
    return jnp.concatenate([in_ref[b, t : t + samples] for b in range(blocks) for t in range(0, length, samples)], 1)


def gradient_kernel(residual_ref, high_ref, low_ref, out_ref):
    samples, cols = out_ref.shape[1:]
    both, high = stacked(joined(residual_ref, samples))
    for c in range(CUBE):
        at = slice(c * cols, (c + 1) * cols)
        wide = dot(both, high_ref[:, at], DOWN)
        out_ref[c] = wide[:samples] + wide[samples:] + dot(high, low_ref[:, at], DOWN)


def gradient_parts(residual, high, low, samples):
    return call(
        gradient_kernel,
        array(CUBE, samples, high.shape[1] // CUBE),
        "gradient",
        6,
        in_specs=[WHOLE] * 3,
        out_specs=WHOLE,
    )(residual, high, low)


def moved_on(state):
    theta_ref, velocity_ref, gradient_ref, scale_ref = state
    velocity = 0.9 * velocity_ref[...] + scale_ref[:, :1] * gradient_ref[...]
    return theta_ref[...] - 0.5 * velocity, velocity


def whole_gradient(own_ref, other_ref, prec_ref, anchor_ref, theta):
    gradient = own_ref[...] + other_ref[...] + prec_ref[...] * (theta - anchor_ref[...])
    return gradient, jnp.sum(gradient * gradient, axis=1, keepdims=True)


def send_gradient(out_ref, gradient, square):
    samples, cols = gradient.shape
    tail = to_lanes(square)
    for c in range(CUBE):
        for t in range(cols // LANES):
            out_ref[c, t * samples : (t + 1) * samples] = gradient[:, t * LANES : (t + 1) * LANES]
        out_ref[c, cols // LANES * samples :] = tail


def first_step_kernel(own_ref, other_ref, prec_ref, anchor_ref, out_ref, gradient_ref):
    gradient, square = whole_gradient(own_ref, other_ref, prec_ref, anchor_ref, anchor_ref[...])
    gradient_ref[...] = gradient
    send_gradient(out_ref, gradient, square)


def next_step_kernel(own_ref, other_ref, prec_ref, anchor_ref, *refs):
    state, (out_ref, gradient_ref, theta_ref, velocity_ref) = refs[:4], refs[4:]
    theta, velocity = moved_on(state)
    theta_ref[...] = theta
    velocity_ref[...] = velocity
    gradient, square = whole_gradient(own_ref, other_ref, prec_ref, anchor_ref, theta)
    gradient_ref[...] = gradient
    send_gradient(out_ref, gradient, square)


def stepped(own, other, prec, anchor, state=()):
    samples, cols = anchor.shape
    outs = 3 if state else 1
    return call(
        next_step_kernel if state else first_step_kernel,
        [array(CUBE, cols // LANES * samples + TAIL, LANES)] + [array(samples, cols)] * outs,
        "next_step" if state else "first_step",
        4,
        in_specs=[WHOLE] * (4 + len(state)),
        out_specs=[WHOLE] * (1 + outs),
    )(own, other, prec, anchor, *state)


def push(parts, flip_high, flip_low, samples):
    def kernel(in_ref, high_ref, low_ref, out_ref):
        both, first = stacked(joined(in_ref, samples))
        tail = jnp.sum(in_ref[:, -TAIL:], axis=0)
        for j in range(CUBE):
            put_part(out_ref, j, both, first, high_ref[j], low_ref[j], tail)

    return call(
        kernel,
        array(CUBE, flip_high.shape[2] // LANES * samples + TAIL, LANES),
        "push",
        6,
        in_specs=[WHOLE] * 3,
        out_specs=WHOLE,
    )(parts, flip_high, flip_low)


def last_kernel(own_ref, other_ref, prec_ref, anchor_ref, *refs):
    state, (squares_ref, gradient_ref, theta_ref, velocity_ref) = refs[:4], refs[4:]
    theta, velocity = moved_on(state)
    theta_ref[...] = theta
    velocity_ref[...] = velocity
    gradient, square = whole_gradient(own_ref, other_ref, prec_ref, anchor_ref, theta)
    gradient_ref[...] = gradient
    squares_ref[...] = jnp.broadcast_to(to_lanes(square)[:1], squares_ref.shape)


def last_gradient(own, other, prec, anchor, state):
    shape = anchor.shape
    return call(
        last_kernel,
        [array(SIDE**3, LANES)] + [array(*shape)] * 3,
        "last_gradient",
        4,
        in_specs=[WHOLE] * 8,
        out_specs=[WHOLE] * 4,
    )(own, other, prec, anchor, *state)


def close(squares, theta, velocity, gradient, clip_level, params):
    samples = theta.shape[0]

    def kernel(squares_ref, theta_ref, velocity_ref, gradient_ref, out_ref):
        row = jnp.sum(squares_ref[...], axis=0, keepdims=True)
        scale = scale_from(row, samples, clip_level, params)
        velocity = 0.9 * velocity_ref[...] + scale * gradient_ref[...]
        out_ref[...] = theta_ref[...] - 0.5 * velocity

    return call(kernel, array(*theta.shape), "close", 4, in_specs=[WHOLE] * 4, out_specs=WHOLE)(
        squares, theta, velocity, gradient
    )


def body(jacobian, targets, anchor, precision):
    samples, col_dev = anchor.shape
    row_dev = jacobian.shape[0]
    params = col_dev * SIDE**3
    clip_level = 0.2 * math.sqrt(row_dev * 2 / params)
    half, pair = own_block()
    at = jnp.reshape(pair * CUBE + half, (1,)).astype(jnp.int32)
    prec = precision[None, :]
    jacobian, at = lax.optimization_barrier((jacobian, at))
    square = exchange(jacobian.reshape(CUBE, row_dev // CUBE, col_dev), SECOND)
    square, theta = lax.optimization_barrier((square, anchor))
    theta = exchange(jnp.broadcast_to(theta[None], (CUBE, samples, col_dev)), SECOND)
    parts, own, high, low, *flips = opened(at, targets, theta, square)
    residual, logits = first_residual(exchange(parts, FIRST), own)
    slope = jnp.zeros_like(logits)
    state = ()
    for step in range(STEPS):
        parts = gradient_parts(exchange(residual, FIRST), high, low, samples)
        gradient = fold(exchange(parts, SECOND))
        other = lax.ppermute(gradient, "rows", [(0, 1), (1, 0)])
        if step + 1 == STEPS:
            break
        parts, gradient, *moved = stepped(gradient, other, prec, anchor, state)
        theta, velocity = moved if moved else (anchor, jnp.zeros_like(anchor))
        parts = exchange(push(exchange(parts, SECOND), *flips, samples), FIRST)
        last = step + 2 == STEPS
        residual, scale, *kept = next_residual(parts, own, logits, slope, samples, clip_level, params, last)
        logits, slope = kept or (None, None)
        state = (theta, velocity, gradient, scale)
    squares, gradient, theta, velocity = last_gradient(gradient, other, prec, anchor, state)
    squares = lax.all_to_all(squares, COLS, split_axis=0, concat_axis=0, tiled=True)
    return close(squares, theta, velocity, gradient, clip_level, params)


def solution(mesh):
    cubes = Mesh(mesh.devices.reshape(2, SIDE, SIDE, SIDE), AXES)
    in_specs = (P("rows", COLS), P(None, "rows"), P(None, COLS), P(COLS))
    out_specs = P(None, COLS)
    return jax.shard_map(body, mesh=cubes, in_specs=in_specs, out_specs=out_specs, check_vma=False)
```

```python
import math

import jax
import jax.numpy as jnp
from jax import lax
from jax.experimental import pallas as pl
from jax.experimental.pallas import tpu as pltpu
from jax.sharding import Mesh
from jax.sharding import PartitionSpec as P

STEPS = 3
SPLIT = (3, 3, 2)
SIDE = 4
CUBE = 8
SHIFT = (1, 1, 0)
AXES = ("rows", "z", "y", "x")
COLS = ("z", "y", "x")
LANES = 128
TAIL = 8
F32 = jnp.float32
BF16 = jnp.bfloat16
ACROSS = (((1,), (1,)), ((), ()))
DOWN = (((1,), (0,)), ((), ()))
WHOLE = pl.BlockSpec(memory_space=pltpu.VMEM)


def place(core, at):
    turned = [(p + core + s) & (SIDE - 1) for p, s in zip(at, SHIFT)]
    half = [((t + 1) >> 1) & 1 for t in turned]
    pair = [t >> 1 for t in turned]
    return walk(half), walk(pair)


def walk(bits):
    a, b, c = bits
    return a * 4 + (a ^ b) * 2 + (a ^ b ^ c)


def cube_groups():
    first, second = {}, {}
    for device in range(2 * SIDE**3):
        core, z, y, x = device // 64, device // 16 % 4, device // 4 % 4, device % 4
        half, pair = place(core, (z, y, x))
        first.setdefault((core, pair), {})[half] = device
        second.setdefault((core, half), {})[pair] = device
    in_order = lambda groups: [[group[k] for k in range(CUBE)] for _, group in sorted(groups.items())]
    return in_order(first), in_order(second)


FIRST, SECOND = cube_groups()


def exchange(x, groups):
    return lax.all_to_all(x, AXES, split_axis=0, concat_axis=0, axis_index_groups=groups, tiled=True)


def own_block():
    return place(lax.axis_index("rows"), [lax.axis_index(a) for a in COLS])


def call(kernel, out_shape, name, mib, **kw):
    return pl.pallas_call(
        kernel,
        out_shape=out_shape,
        name=name,
        compiler_params=pltpu.CompilerParams(vmem_limit_bytes=mib << 20),
        **kw,
    )


def array(*shape, dtype=F32):
    return jax.ShapeDtypeStruct(shape, dtype)


def halves(x):
    high = x.astype(BF16)
    return high, (x - high.astype(F32)).astype(BF16)


def dot(a, b, dims):
    return lax.dot_general(a, b, dims, preferred_element_type=F32)


def diagonal(samples):
    shape = (samples, LANES)
    return lax.broadcasted_iota(jnp.int32, shape, 0) == lax.broadcasted_iota(jnp.int32, shape, 1)


def to_lanes(column):
    samples = column.shape[0]
    row = jnp.sum(jnp.where(diagonal(samples), column, 0.0), axis=0, keepdims=True)
    return jnp.broadcast_to(row, (TAIL, LANES))


def to_column(row, samples):
    return jnp.sum(jnp.where(diagonal(samples), row, 0.0), axis=1, keepdims=True)


def stacked(x):
    high, low = halves(x)
    return jnp.concatenate([high, low], 0), high


def put_part(out_ref, j, both, high, flip_high, flip_low, tail):
    samples = high.shape[0]
    tiles = flip_high.shape[1] // LANES
    wide = dot(both, flip_high, DOWN)
    logits = wide[:samples] + wide[samples:] + dot(high, flip_low, DOWN)
    for t in range(tiles):
        out_ref[j, t * samples : (t + 1) * samples] = logits[:, t * LANES : (t + 1) * LANES]
    out_ref[j, tiles * samples :] = tail


def split_kernel(jac_ref, high_ref, low_ref, flip_high_ref, flip_low_ref):
    j = pl.program_id(0)
    _, part, cols = jac_ref.shape
    rows = pl.ds(pl.multiple_of(j * part, part), part)
    for c in range(CUBE):
        jac_high, jac_low = halves(jac_ref[c])
        at = slice(c * cols, (c + 1) * cols)
        high_ref[rows, at] = jac_high
        low_ref[rows, at] = jac_low
        flip_high_ref[j, at] = jnp.transpose(jac_high)
        flip_low_ref[j, at] = jnp.transpose(jac_low)


def split(jacobian, first, parts):
    _, rows, cols = jacobian.shape
    part = rows // CUBE
    wide = CUBE * cols
    return call(
        split_kernel,
        [array(parts * part, wide, dtype=BF16)] * 2 + [array(parts, wide, part, dtype=BF16)] * 2,
        "split",
        12,
        grid=(parts,),
        in_specs=[pl.BlockSpec((CUBE, part, cols), lambda j: (0, j + first, 0))],
        out_specs=[WHOLE] * 4,
    )(in_hbm(jacobian))


def beside_kernel(own_ref, other_ref, out_ref):
    members = own_ref.shape[0]
    out_ref[:members] = own_ref[...]
    out_ref[members:] = other_ref[...]


def beside(own, other):
    shape = (2 * own.shape[0], *own.shape[1:])
    return call(beside_kernel, array(*shape), "beside", 4, in_specs=[WHOLE] * 2, out_specs=WHOLE)(own, other)


def across(bit):
    pairs = []
    for group in SECOND:
        for k in range(CUBE):
            corner = (k ^ (k >> 1)) ^ (1 << bit)
            pairs.append((group[k], group[walk((corner >> 2, corner >> 1 & 1, corner & 1))]))
    return pairs


def open_kernel(at_ref, targets_ref, theta_ref, *refs):
    flips, (out_ref, own_ref, both_ref) = refs[:-3], refs[-3:]
    samples, cols = theta_ref.shape[1:]
    for t in range(targets_ref.shape[1] // LANES):
        own_ref[t * samples : (t + 1) * samples] = targets_ref[:, t * LANES : (t + 1) * LANES]
    for c in range(CUBE):
        theta = theta_ref[(c ^ (c >> 1)) ^ at_ref[1]]
        both_ref[:, c * cols : (c + 1) * cols], _ = stacked(theta)
    both = both_ref[...]
    put_all(out_ref, both, both[:samples], flips, jnp.zeros((TAIL, LANES), F32))


def put_all(out_ref, both, high, flips, tail):
    j = 0
    for high_ref, low_ref in zip(flips[::2], flips[1::2]):
        for k in range(high_ref.shape[0]):
            put_part(out_ref, j, both, high, high_ref[k], low_ref[k], tail)
            j += 1


def opened(at, targets, theta, flips):
    samples, cols = theta.shape[1:]
    part = flips[0].shape[2]
    length = part // LANES * samples
    return pl.pallas_call(
        open_kernel,
        name="opened",
        out_shape=[array(CUBE, length + TAIL, LANES), array(length, LANES)],
        grid_spec=pltpu.PrefetchScalarGridSpec(
            num_scalar_prefetch=1,
            grid=(1,),
            in_specs=[pl.BlockSpec((samples, part), lambda j, at: (0, at[0]))] + [WHOLE] * (1 + len(flips)),
            out_specs=[WHOLE] * 2,
            scratch_shapes=[pltpu.VMEM((2 * samples, CUBE * cols), BF16)],
        ),
        compiler_params=pltpu.CompilerParams(vmem_limit_bytes=6 << 20),
    )(at, in_hbm(targets), theta, *flips)


def in_hbm(x):
    return pltpu.with_memory_space_constraint(x, pltpu.HBM)


def fold_kernel(in_ref, out_ref):
    out_ref[...] = jnp.sum(in_ref[...], axis=0)


def fold(parts):
    return call(fold_kernel, array(*parts.shape[1:]), "fold", 4, in_specs=[WHOLE], out_specs=WHOLE)(parts)


def scale_from(row, samples, clip_level, params):
    squares = to_column(row, samples)
    return jnp.minimum(1.0, clip_level / jnp.sqrt(squares / params + 1e-06))


def residual_to(out_ref, logits, targets):
    residual = jax.nn.sigmoid(logits) - targets
    for i in range(CUBE):
        out_ref[i] = residual


def first_residual_kernel(in_ref, targets_ref, residual_ref, logits_ref):
    logits = jnp.sum(in_ref[:, : targets_ref.shape[0]], axis=0)
    logits_ref[...] = logits
    residual_to(residual_ref, logits, targets_ref[...])


def first_residual(parts, targets):
    return call(
        first_residual_kernel,
        [array(CUBE, *targets.shape), array(*targets.shape)],
        "first_residual",
        4,
        in_specs=[WHOLE] * 2,
        out_specs=[WHOLE] * 2,
    )(parts, targets)


def next_residual(parts, targets, logits, slope, samples, clip_level, params, last):
    def kernel(in_ref, targets_ref, logits_ref, slope_ref, residual_ref, scale_ref, *kept):
        length = targets_ref.shape[0]
        row = jnp.sum(in_ref[:, length:], axis=0)[:1]
        scale = scale_from(row, samples, clip_level, params)
        scale_ref[...] = jnp.broadcast_to(scale, scale_ref.shape)
        moved = jnp.sum(in_ref[:, :length], axis=0)
        every = jnp.concatenate([scale] * (length // samples), 0)
        slope = 0.9 * slope_ref[...] + every * moved
        logits = logits_ref[...] - 0.5 * slope
        if kept:
            kept[0][...] = logits
            kept[1][...] = slope
        residual_to(residual_ref, logits, targets_ref[...])

    shape = targets.shape
    kept = 0 if last else 2
    return call(
        kernel,
        [array(CUBE, *shape), array(samples, LANES)] + [array(*shape)] * kept,
        "last_residual" if last else "next_residual",
        4,
        in_specs=[WHOLE] * 4,
        out_specs=[WHOLE] * (2 + kept),
    )(parts, targets, logits, slope)


def joined(in_ref, samples):
    blocks, length = in_ref.shape[0], in_ref.shape[1] // samples * samples
    return jnp.concatenate([in_ref[b, t : t + samples] for b in range(blocks) for t in range(0, length, samples)], 1)


def gradient_kernel(residual_ref, *refs):
    jac, out_ref = refs[:-1], refs[-1]
    samples, cols = out_ref.shape[1:]
    both, high = stacked(joined(residual_ref, samples))
    for c in range(CUBE):
        at = slice(c * cols, (c + 1) * cols)
        total, row = 0.0, 0
        for high_ref, low_ref in zip(jac[::2], jac[1::2]):
            rows = slice(row, row + high_ref.shape[0])
            wide = dot(both[:, rows], high_ref[:, at], DOWN)
            total += wide[:samples] + wide[samples:] + dot(high[:, rows], low_ref[:, at], DOWN)
            row = rows.stop
        out_ref[c] = total


def gradient_parts(residual, jac, samples):
    return call(
        gradient_kernel,
        array(CUBE, samples, jac[0].shape[1] // CUBE),
        "gradient",
        6,
        in_specs=[WHOLE] * (1 + len(jac)),
        out_specs=WHOLE,
    )(residual, *jac)


def moved_on(state):
    theta_ref, velocity_ref, gradient_ref, scale_ref = state
    velocity = 0.9 * velocity_ref[...] + scale_ref[:, :1] * gradient_ref[...]
    return theta_ref[...] - 0.5 * velocity, velocity


def whole_gradient(own_ref, other_ref, prec_ref, anchor_ref, theta):
    gradient = own_ref[...] + other_ref[...] + prec_ref[...] * (theta - anchor_ref[...])
    return gradient, jnp.sum(gradient * gradient, axis=1, keepdims=True)


def send_gradient(out_ref, gradient, square):
    samples, cols = gradient.shape
    tail = to_lanes(square)
    for c in range(CUBE):
        for t in range(cols // LANES):
            out_ref[c, t * samples : (t + 1) * samples] = gradient[:, t * LANES : (t + 1) * LANES]
        out_ref[c, cols // LANES * samples :] = tail


def first_step_kernel(own_ref, other_ref, prec_ref, anchor_ref, out_ref, gradient_ref):
    gradient, square = whole_gradient(own_ref, other_ref, prec_ref, anchor_ref, anchor_ref[...])
    gradient_ref[...] = gradient
    send_gradient(out_ref, gradient, square)


def next_step_kernel(own_ref, other_ref, prec_ref, anchor_ref, *refs):
    state, (out_ref, gradient_ref, theta_ref, velocity_ref) = refs[:4], refs[4:]
    theta, velocity = moved_on(state)
    theta_ref[...] = theta
    velocity_ref[...] = velocity
    gradient, square = whole_gradient(own_ref, other_ref, prec_ref, anchor_ref, theta)
    gradient_ref[...] = gradient
    send_gradient(out_ref, gradient, square)


def stepped(own, other, prec, anchor, state=()):
    samples, cols = anchor.shape
    outs = 3 if state else 1
    return call(
        next_step_kernel if state else first_step_kernel,
        [array(CUBE, cols // LANES * samples + TAIL, LANES)] + [array(samples, cols)] * outs,
        "next_step" if state else "first_step",
        4,
        in_specs=[WHOLE] * (4 + len(state)),
        out_specs=[WHOLE] * (1 + outs),
    )(own, other, prec, anchor, *state)


def push(parts, flips, samples):
    def kernel(in_ref, *refs):
        both, first = stacked(joined(in_ref, samples))
        put_all(refs[-1], both, first, refs[:-1], jnp.sum(in_ref[:, -TAIL:], axis=0))

    return call(
        kernel,
        array(CUBE, flips[0].shape[2] // LANES * samples + TAIL, LANES),
        "push",
        6,
        in_specs=[WHOLE] * (1 + len(flips)),
        out_specs=WHOLE,
    )(parts, *flips)


def last_kernel(own_ref, other_ref, prec_ref, anchor_ref, *refs):
    state, (squares_ref, gradient_ref, theta_ref, velocity_ref) = refs[:4], refs[4:]
    theta, velocity = moved_on(state)
    theta_ref[...] = theta
    velocity_ref[...] = velocity
    gradient, square = whole_gradient(own_ref, other_ref, prec_ref, anchor_ref, theta)
    gradient_ref[...] = gradient
    squares_ref[...] = jnp.broadcast_to(to_lanes(square)[:1], squares_ref.shape)


def last_gradient(own, other, prec, anchor, state):
    shape = anchor.shape
    return call(
        last_kernel,
        [array(SIDE**3, LANES)] + [array(*shape)] * 3,
        "last_gradient",
        4,
        in_specs=[WHOLE] * 8,
        out_specs=[WHOLE] * 4,
    )(own, other, prec, anchor, *state)


def close(squares, theta, velocity, gradient, clip_level, params):
    samples = theta.shape[0]

    def kernel(squares_ref, theta_ref, velocity_ref, gradient_ref, out_ref):
        row = jnp.sum(squares_ref[...], axis=0, keepdims=True)
        scale = scale_from(row, samples, clip_level, params)
        velocity = 0.9 * velocity_ref[...] + scale * gradient_ref[...]
        out_ref[...] = theta_ref[...] - 0.5 * velocity

    return call(kernel, array(*theta.shape), "close", 4, in_specs=[WHOLE] * 4, out_specs=WHOLE)(
        squares, theta, velocity, gradient
    )


def body(jacobian, targets, anchor, precision):
    samples, col_dev = anchor.shape
    row_dev = jacobian.shape[0]
    params = col_dev * SIDE**3
    clip_level = 0.2 * math.sqrt(row_dev * 2 / params)
    half, pair = own_block()
    at = jnp.stack([pair * CUBE + half, pair ^ (pair >> 1)]).astype(jnp.int32)
    prec = precision[None, :]
    jacobian, at = lax.optimization_barrier((jacobian, at))
    square = exchange(jacobian.reshape(CUBE, row_dev // CUBE, col_dev), SECOND)
    square, theta = lax.optimization_barrier((square, anchor[None]))
    jac, flips, first = [], [], 0
    for bit, parts in enumerate(SPLIT):
        other = lax.ppermute(theta, AXES, across(bit))
        other, square, high, low, *flip = lax.optimization_barrier((other, square, *split(square, first, parts)))
        theta = beside(theta, other)
        jac, flips, first = [*jac, high, low], [*flips, *flip], first + parts
    parts, own = opened(at, targets, theta, flips)
    residual, logits = first_residual(exchange(parts, FIRST), own)
    slope = jnp.zeros_like(logits)
    state = ()
    for step in range(STEPS):
        parts = gradient_parts(exchange(residual, FIRST), jac, samples)
        gradient = fold(exchange(parts, SECOND))
        other = lax.ppermute(gradient, "rows", [(0, 1), (1, 0)])
        if step + 1 == STEPS:
            break
        parts, gradient, *moved = stepped(gradient, other, prec, anchor, state)
        theta, velocity = moved if moved else (anchor, jnp.zeros_like(anchor))
        parts = exchange(push(exchange(parts, SECOND), flips, samples), FIRST)
        last = step + 2 == STEPS
        residual, scale, *kept = next_residual(parts, own, logits, slope, samples, clip_level, params, last)
        logits, slope = kept or (None, None)
        state = (theta, velocity, gradient, scale)
    squares, gradient, theta, velocity = last_gradient(gradient, other, prec, anchor, state)
    squares = lax.all_to_all(squares, COLS, split_axis=0, concat_axis=0, tiled=True)
    return close(squares, theta, velocity, gradient, clip_level, params)


def solution(mesh):
    cubes = Mesh(mesh.devices.reshape(2, SIDE, SIDE, SIDE), AXES)
    in_specs = (P("rows", COLS), P(None, "rows"), P(None, COLS), P(COLS))
    out_specs = P(None, COLS)
    return jax.shard_map(body, mesh=cubes, in_specs=in_specs, out_specs=out_specs, check_vma=False)
```

```python
import math

import jax
import jax.numpy as jnp
from jax import lax
from jax.experimental import pallas as pl
from jax.experimental.pallas import tpu as pltpu
from jax.sharding import Mesh
from jax.sharding import PartitionSpec as P

STEPS = 3
SPLIT = (2, 3, 3)
SIDE = 4
CUBE = 8
SHIFT = (1, 1, 0)
AXES = ("rows", "z", "y", "x")
COLS = ("z", "y", "x")
LANES = 128
TAIL = 8
F32 = jnp.float32
BF16 = jnp.bfloat16
ACROSS = (((1,), (1,)), ((), ()))
DOWN = (((1,), (0,)), ((), ()))
WHOLE = pl.BlockSpec(memory_space=pltpu.VMEM)


def place(core, at):
    turned = [(p + core + s) & (SIDE - 1) for p, s in zip(at, SHIFT)]
    half = [((t + 1) >> 1) & 1 for t in turned]
    pair = [t >> 1 for t in turned]
    return walk(half), walk(pair)


def walk(bits):
    a, b, c = bits
    return a * 4 + (a ^ b) * 2 + (a ^ b ^ c)


def cube_groups():
    first, second = {}, {}
    for device in range(2 * SIDE**3):
        core, z, y, x = device // 64, device // 16 % 4, device // 4 % 4, device % 4
        half, pair = place(core, (z, y, x))
        first.setdefault((core, pair), {})[half] = device
        second.setdefault((core, half), {})[pair] = device
    in_order = lambda groups: [[group[k] for k in range(CUBE)] for _, group in sorted(groups.items())]
    return in_order(first), in_order(second)


FIRST, SECOND = cube_groups()


def exchange(x, groups):
    return lax.all_to_all(x, AXES, split_axis=0, concat_axis=0, axis_index_groups=groups, tiled=True)


def own_block():
    return place(lax.axis_index("rows"), [lax.axis_index(a) for a in COLS])


def call(kernel, out_shape, name, mib, **kw):
    return pl.pallas_call(
        kernel,
        out_shape=out_shape,
        name=name,
        compiler_params=pltpu.CompilerParams(vmem_limit_bytes=mib << 20),
        **kw,
    )


def array(*shape, dtype=F32):
    return jax.ShapeDtypeStruct(shape, dtype)


def halves(x):
    high = x.astype(BF16)
    return high, (x - high.astype(F32)).astype(BF16)


def dot(a, b, dims):
    return lax.dot_general(a, b, dims, preferred_element_type=F32)


def diagonal(samples):
    shape = (samples, LANES)
    return lax.broadcasted_iota(jnp.int32, shape, 0) == lax.broadcasted_iota(jnp.int32, shape, 1)


def to_lanes(column):
    samples = column.shape[0]
    row = jnp.sum(jnp.where(diagonal(samples), column, 0.0), axis=0, keepdims=True)
    return jnp.broadcast_to(row, (TAIL, LANES))


def to_column(row, samples):
    return jnp.sum(jnp.where(diagonal(samples), row, 0.0), axis=1, keepdims=True)


def stacked(x):
    high, low = halves(x)
    return jnp.concatenate([high, low], 0), high


def put_part(out_ref, j, both, high, flip_high, flip_low, tail):
    samples = high.shape[0]
    tiles = flip_high.shape[1] // LANES
    wide = dot(both, flip_high, DOWN)
    logits = wide[:samples] + wide[samples:] + dot(high, flip_low, DOWN)
    for t in range(tiles):
        out_ref[j, t * samples : (t + 1) * samples] = logits[:, t * LANES : (t + 1) * LANES]
    out_ref[j, tiles * samples :] = tail


def split_kernel(at_ref, jac_ref, *refs):
    if len(refs) > 4:
        targets_ref, *refs, own_ref = refs
        samples = targets_ref.shape[0]
        for t in range(targets_ref.shape[1] // LANES):
            own_ref[t * samples : (t + 1) * samples] = targets_ref[:, t * LANES : (t + 1) * LANES]
    high_ref, low_ref, flip_high_ref, flip_low_ref = refs
    j = pl.program_id(0)
    _, part, cols = jac_ref.shape
    rows = pl.ds(pl.multiple_of(j * part, part), part)
    for c in range(CUBE):
        jac_high, jac_low = halves(jac_ref[c])
        at = slice(c * cols, (c + 1) * cols)
        high_ref[rows, at] = jac_high
        low_ref[rows, at] = jac_low
        flip_high_ref[j, at] = jnp.transpose(jac_high)
        flip_low_ref[j, at] = jnp.transpose(jac_low)


def split(at, jacobian, first, parts, targets=()):
    _, rows, cols = jacobian.shape
    part = rows // CUBE
    wide = CUBE * cols
    samples = [t.shape[0] for t in targets]
    return pl.pallas_call(
        split_kernel,
        name="split",
        out_shape=[array(parts * part, wide, dtype=BF16)] * 2
        + [array(parts, wide, part, dtype=BF16)] * 2
        + [array(part // LANES * n, LANES) for n in samples],
        grid_spec=pltpu.PrefetchScalarGridSpec(
            num_scalar_prefetch=1,
            grid=(parts,),
            in_specs=[pl.BlockSpec((CUBE, part, cols), lambda j, at: (0, j + first, 0))]
            + [pl.BlockSpec((n, part), lambda j, at: (0, at[0])) for n in samples],
            out_specs=[WHOLE] * (4 + len(samples)),
        ),
        compiler_params=pltpu.CompilerParams(vmem_limit_bytes=12 << 20),
    )(at, in_hbm(jacobian), *(in_hbm(t) for t in targets))


def beside_kernel(own_ref, other_ref, out_ref):
    members = own_ref.shape[0]
    out_ref[:members] = own_ref[...]
    out_ref[members:] = other_ref[...]


def beside(own, other):
    shape = (2 * own.shape[0], *own.shape[1:])
    return call(beside_kernel, array(*shape), "beside", 4, in_specs=[WHOLE] * 2, out_specs=WHOLE)(own, other)


def across(bit):
    pairs = []
    for group in SECOND:
        for k in range(CUBE):
            corner = (k ^ (k >> 1)) ^ (1 << bit)
            pairs.append((group[k], group[walk((corner >> 2, corner >> 1 & 1, corner & 1))]))
    return pairs


def open_kernel(at_ref, theta_ref, *refs):
    flips, (out_ref, both_ref) = refs[:-2], refs[-2:]
    samples, cols = theta_ref.shape[1:]
    for c in range(CUBE):
        theta = theta_ref[(c ^ (c >> 1)) ^ at_ref[1]]
        both_ref[:, c * cols : (c + 1) * cols], _ = stacked(theta)
    both = both_ref[...]
    put_all(out_ref, both, both[:samples], flips, jnp.zeros((TAIL, LANES), F32))


def put_all(out_ref, both, high, flips, tail):
    j = 0
    for high_ref, low_ref in zip(flips[::2], flips[1::2]):
        for k in range(high_ref.shape[0]):
            put_part(out_ref, j, both, high, high_ref[k], low_ref[k], tail)
            j += 1


def opened(at, theta, flips):
    samples, cols = theta.shape[1:]
    length = flips[0].shape[2] // LANES * samples
    return call(
        open_kernel,
        array(CUBE, length + TAIL, LANES),
        "opened",
        6,
        in_specs=[pl.BlockSpec(memory_space=pltpu.SMEM)] + [WHOLE] * (1 + len(flips)),
        out_specs=WHOLE,
        scratch_shapes=[pltpu.VMEM((2 * samples, CUBE * cols), BF16)],
    )(at, theta, *flips)


def in_hbm(x):
    return pltpu.with_memory_space_constraint(x, pltpu.HBM)


def fold_kernel(in_ref, out_ref):
    out_ref[...] = jnp.sum(in_ref[...], axis=0)


def fold(parts):
    return call(fold_kernel, array(*parts.shape[1:]), "fold", 4, in_specs=[WHOLE], out_specs=WHOLE)(parts)


def scale_from(row, samples, clip_level, params):
    squares = to_column(row, samples)
    return jnp.minimum(1.0, clip_level / jnp.sqrt(squares / params + 1e-06))


def residual_to(out_ref, logits, targets):
    residual = jax.nn.sigmoid(logits) - targets
    for i in range(CUBE):
        out_ref[i] = residual


def first_residual_kernel(in_ref, targets_ref, residual_ref, logits_ref):
    logits = jnp.sum(in_ref[:, : targets_ref.shape[0]], axis=0)
    logits_ref[...] = logits
    residual_to(residual_ref, logits, targets_ref[...])


def first_residual(parts, targets):
    return call(
        first_residual_kernel,
        [array(CUBE, *targets.shape), array(*targets.shape)],
        "first_residual",
        4,
        in_specs=[WHOLE] * 2,
        out_specs=[WHOLE] * 2,
    )(parts, targets)


def next_residual(parts, targets, logits, slope, samples, clip_level, params, last):
    def kernel(in_ref, targets_ref, logits_ref, slope_ref, residual_ref, scale_ref, *kept):
        length = targets_ref.shape[0]
        row = jnp.sum(in_ref[:, length:], axis=0)[:1]
        scale = scale_from(row, samples, clip_level, params)
        scale_ref[...] = jnp.broadcast_to(scale, scale_ref.shape)
        moved = jnp.sum(in_ref[:, :length], axis=0)
        every = jnp.concatenate([scale] * (length // samples), 0)
        slope = 0.9 * slope_ref[...] + every * moved
        logits = logits_ref[...] - 0.5 * slope
        if kept:
            kept[0][...] = logits
            kept[1][...] = slope
        residual_to(residual_ref, logits, targets_ref[...])

    shape = targets.shape
    kept = 0 if last else 2
    return call(
        kernel,
        [array(CUBE, *shape), array(samples, LANES)] + [array(*shape)] * kept,
        "last_residual" if last else "next_residual",
        4,
        in_specs=[WHOLE] * 4,
        out_specs=[WHOLE] * (2 + kept),
    )(parts, targets, logits, slope)


def joined(in_ref, samples):
    blocks, length = in_ref.shape[0], in_ref.shape[1] // samples * samples
    return jnp.concatenate([in_ref[b, t : t + samples] for b in range(blocks) for t in range(0, length, samples)], 1)


def gradient_kernel(residual_ref, *refs):
    jac, out_ref = refs[:-1], refs[-1]
    samples, cols = out_ref.shape[1:]
    both, high = stacked(joined(residual_ref, samples))
    for c in range(CUBE):
        at = slice(c * cols, (c + 1) * cols)
        total, row = 0.0, 0
        for high_ref, low_ref in zip(jac[::2], jac[1::2]):
            rows = slice(row, row + high_ref.shape[0])
            wide = dot(both[:, rows], high_ref[:, at], DOWN)
            total += wide[:samples] + wide[samples:] + dot(high[:, rows], low_ref[:, at], DOWN)
            row = rows.stop
        out_ref[c] = total


def gradient_parts(residual, jac, samples):
    return call(
        gradient_kernel,
        array(CUBE, samples, jac[0].shape[1] // CUBE),
        "gradient",
        6,
        in_specs=[WHOLE] * (1 + len(jac)),
        out_specs=WHOLE,
    )(residual, *jac)


def moved_on(state):
    theta_ref, velocity_ref, gradient_ref, scale_ref = state
    velocity = 0.9 * velocity_ref[...] + scale_ref[:, :1] * gradient_ref[...]
    return theta_ref[...] - 0.5 * velocity, velocity


def whole_gradient(own_ref, other_ref, prec_ref, anchor_ref, theta):
    gradient = own_ref[...] + other_ref[...] + prec_ref[...] * (theta - anchor_ref[...])
    return gradient, jnp.sum(gradient * gradient, axis=1, keepdims=True)


def send_gradient(out_ref, gradient, square):
    samples, cols = gradient.shape
    tail = to_lanes(square)
    for c in range(CUBE):
        for t in range(cols // LANES):
            out_ref[c, t * samples : (t + 1) * samples] = gradient[:, t * LANES : (t + 1) * LANES]
        out_ref[c, cols // LANES * samples :] = tail


def first_step_kernel(own_ref, other_ref, prec_ref, anchor_ref, out_ref, gradient_ref):
    gradient, square = whole_gradient(own_ref, other_ref, prec_ref, anchor_ref, anchor_ref[...])
    gradient_ref[...] = gradient
    send_gradient(out_ref, gradient, square)


def next_step_kernel(own_ref, other_ref, prec_ref, anchor_ref, *refs):
    state, (out_ref, gradient_ref, theta_ref, velocity_ref) = refs[:4], refs[4:]
    theta, velocity = moved_on(state)
    theta_ref[...] = theta
    velocity_ref[...] = velocity
    gradient, square = whole_gradient(own_ref, other_ref, prec_ref, anchor_ref, theta)
    gradient_ref[...] = gradient
    send_gradient(out_ref, gradient, square)


def stepped(own, other, prec, anchor, state=()):
    samples, cols = anchor.shape
    outs = 3 if state else 1
    return call(
        next_step_kernel if state else first_step_kernel,
        [array(CUBE, cols // LANES * samples + TAIL, LANES)] + [array(samples, cols)] * outs,
        "next_step" if state else "first_step",
        4,
        in_specs=[WHOLE] * (4 + len(state)),
        out_specs=[WHOLE] * (1 + outs),
    )(own, other, prec, anchor, *state)


def push(parts, flips, samples):
    def kernel(in_ref, *refs):
        both, first = stacked(joined(in_ref, samples))
        put_all(refs[-1], both, first, refs[:-1], jnp.sum(in_ref[:, -TAIL:], axis=0))

    return call(
        kernel,
        array(CUBE, flips[0].shape[2] // LANES * samples + TAIL, LANES),
        "push",
        6,
        in_specs=[WHOLE] * (1 + len(flips)),
        out_specs=WHOLE,
    )(parts, *flips)


def last_kernel(own_ref, other_ref, prec_ref, anchor_ref, *refs):
    state, (squares_ref, gradient_ref, theta_ref, velocity_ref) = refs[:4], refs[4:]
    theta, velocity = moved_on(state)
    theta_ref[...] = theta
    velocity_ref[...] = velocity
    gradient, square = whole_gradient(own_ref, other_ref, prec_ref, anchor_ref, theta)
    gradient_ref[...] = gradient
    squares_ref[...] = jnp.broadcast_to(to_lanes(square)[:1], squares_ref.shape)


def last_gradient(own, other, prec, anchor, state):
    shape = anchor.shape
    return call(
        last_kernel,
        [array(SIDE**3, LANES)] + [array(*shape)] * 3,
        "last_gradient",
        4,
        in_specs=[WHOLE] * 8,
        out_specs=[WHOLE] * 4,
    )(own, other, prec, anchor, *state)


def close(squares, theta, velocity, gradient, clip_level, params):
    samples = theta.shape[0]

    def kernel(squares_ref, theta_ref, velocity_ref, gradient_ref, out_ref):
        row = jnp.sum(squares_ref[...], axis=0, keepdims=True)
        scale = scale_from(row, samples, clip_level, params)
        velocity = 0.9 * velocity_ref[...] + scale * gradient_ref[...]
        out_ref[...] = theta_ref[...] - 0.5 * velocity

    return call(kernel, array(*theta.shape), "close", 4, in_specs=[WHOLE] * 4, out_specs=WHOLE)(
        squares, theta, velocity, gradient
    )


def body(jacobian, targets, anchor, precision):
    samples, col_dev = anchor.shape
    row_dev = jacobian.shape[0]
    params = col_dev * SIDE**3
    clip_level = 0.2 * math.sqrt(row_dev * 2 / params)
    half, pair = own_block()
    at = jnp.stack([pair * CUBE + half, pair ^ (pair >> 1)]).astype(jnp.int32)
    prec = precision[None, :]
    jacobian, at = lax.optimization_barrier((jacobian, at))
    square = exchange(jacobian.reshape(CUBE, row_dev // CUBE, col_dev), SECOND)
    square, theta = lax.optimization_barrier((square, anchor[None]))
    jac, flips, first = [], [], 0
    for bit, parts in enumerate(SPLIT):
        other = lax.ppermute(theta, AXES, across(bit))
        pieces = split(at, square, first, parts, () if bit else (targets,))
        other, square, high, low, *flip = lax.optimization_barrier((other, square, *pieces))
        if not bit:
            *flip, own = flip
        theta = beside(theta, other)
        jac, flips, first = [*jac, high, low], [*flips, *flip], first + parts
    parts = opened(at, theta, flips)
    residual, logits = first_residual(exchange(parts, FIRST), own)
    slope = jnp.zeros_like(logits)
    state = ()
    for step in range(STEPS):
        parts = gradient_parts(exchange(residual, FIRST), jac, samples)
        gradient = fold(exchange(parts, SECOND))
        other = lax.ppermute(gradient, "rows", [(0, 1), (1, 0)])
        if step + 1 == STEPS:
            break
        parts, gradient, *moved = stepped(gradient, other, prec, anchor, state)
        theta, velocity = moved if moved else (anchor, jnp.zeros_like(anchor))
        parts = exchange(push(exchange(parts, SECOND), flips, samples), FIRST)
        last = step + 2 == STEPS
        residual, scale, *kept = next_residual(parts, own, logits, slope, samples, clip_level, params, last)
        logits, slope = kept or (None, None)
        state = (theta, velocity, gradient, scale)
    squares, gradient, theta, velocity = last_gradient(gradient, other, prec, anchor, state)
    squares = lax.all_to_all(squares, COLS, split_axis=0, concat_axis=0, tiled=True)
    return close(squares, theta, velocity, gradient, clip_level, params)


def solution(mesh):
    cubes = Mesh(mesh.devices.reshape(2, SIDE, SIDE, SIDE), AXES)
    in_specs = (P("rows", COLS), P(None, "rows"), P(None, COLS), P(COLS))
    out_specs = P(None, COLS)
    return jax.shard_map(body, mesh=cubes, in_specs=in_specs, out_specs=out_specs, check_vma=False)
```

```python
import math

import jax
import jax.numpy as jnp
from jax import lax
from jax.experimental import pallas as pl
from jax.experimental.pallas import tpu as pltpu
from jax.sharding import Mesh
from jax.sharding import PartitionSpec as P

STEPS = 3
SPLIT = (2, 3, 3)
SIDE = 4
CUBE = 8
SHIFT = (1, 1, 0)
AXES = ("rows", "z", "y", "x")
COLS = ("z", "y", "x")
LANES = 128
TAIL = 8
F32 = jnp.float32
BF16 = jnp.bfloat16
ACROSS = (((1,), (1,)), ((), ()))
DOWN = (((1,), (0,)), ((), ()))
WHOLE = pl.BlockSpec(memory_space=pltpu.VMEM)


def place(core, at):
    turned = [(p + core + s) & (SIDE - 1) for p, s in zip(at, SHIFT)]
    half = [((t + 1) >> 1) & 1 for t in turned]
    pair = [t >> 1 for t in turned]
    return number(half), number(pair)


def number(bits):
    a, b, c = bits
    return (a ^ b) * 4 + (a ^ c) * 2 + a


def corner_of(k):
    return (k & 1) * 4 + ((k >> 1) ^ (3 * (k & 1)))


def cube_groups():
    first, second = {}, {}
    for device in range(2 * SIDE**3):
        core, z, y, x = device // 64, device // 16 % 4, device // 4 % 4, device % 4
        half, pair = place(core, (z, y, x))
        first.setdefault((core, pair), {})[half] = device
        second.setdefault((core, half), {})[pair] = device
    in_order = lambda groups: [[group[k] for k in range(CUBE)] for _, group in sorted(groups.items())]
    return in_order(first), in_order(second)


FIRST, SECOND = cube_groups()


def exchange(x, groups):
    return lax.all_to_all(x, AXES, split_axis=0, concat_axis=0, axis_index_groups=groups, tiled=True)


def own_block():
    return place(lax.axis_index("rows"), [lax.axis_index(a) for a in COLS])


def call(kernel, out_shape, name, mib, **kw):
    return pl.pallas_call(
        kernel,
        out_shape=out_shape,
        name=name,
        compiler_params=pltpu.CompilerParams(vmem_limit_bytes=mib << 20),
        **kw,
    )


def array(*shape, dtype=F32):
    return jax.ShapeDtypeStruct(shape, dtype)


def halves(x):
    high = x.astype(BF16)
    return high, (x - high.astype(F32)).astype(BF16)


def dot(a, b, dims):
    return lax.dot_general(a, b, dims, preferred_element_type=F32)


def diagonal(samples):
    shape = (samples, LANES)
    return lax.broadcasted_iota(jnp.int32, shape, 0) == lax.broadcasted_iota(jnp.int32, shape, 1)


def to_lanes(column):
    samples = column.shape[0]
    row = jnp.sum(jnp.where(diagonal(samples), column, 0.0), axis=0, keepdims=True)
    return jnp.broadcast_to(row, (TAIL, LANES))


def to_column(row, samples):
    return jnp.sum(jnp.where(diagonal(samples), row, 0.0), axis=1, keepdims=True)


def stacked(x):
    high, low = halves(x)
    return jnp.concatenate([high, low], 0), high


def put_part(out_ref, j, both, high, flip_high, flip_low, tail):
    samples = high.shape[0]
    tiles = flip_high.shape[1] // LANES
    wide = dot(both, flip_high, DOWN)
    logits = wide[:samples] + wide[samples:] + dot(high, flip_low, DOWN)
    for t in range(tiles):
        out_ref[j, t * samples : (t + 1) * samples] = logits[:, t * LANES : (t + 1) * LANES]
    out_ref[j, tiles * samples :] = tail


def split_kernel(at_ref, jac_ref, *refs):
    if len(refs) > 4:
        targets_ref, *refs, own_ref = refs
        samples = targets_ref.shape[0]
        for t in range(targets_ref.shape[1] // LANES):
            own_ref[t * samples : (t + 1) * samples] = targets_ref[:, t * LANES : (t + 1) * LANES]
    high_ref, low_ref, flip_high_ref, flip_low_ref = refs
    j = pl.program_id(0)
    _, part, cols = jac_ref.shape
    rows = pl.ds(pl.multiple_of(j * part, part), part)
    for c in range(CUBE):
        jac_high, jac_low = halves(jac_ref[c])
        at = slice(c * cols, (c + 1) * cols)
        high_ref[rows, at] = jac_high
        low_ref[rows, at] = jac_low
        flip_high_ref[j, at] = jnp.transpose(jac_high)
        flip_low_ref[j, at] = jnp.transpose(jac_low)


def split(at, jacobian, first, parts, targets=()):
    _, rows, cols = jacobian.shape
    part = rows // CUBE
    wide = CUBE * cols
    samples = [t.shape[0] for t in targets]
    return pl.pallas_call(
        split_kernel,
        name="split",
        out_shape=[array(parts * part, wide, dtype=BF16)] * 2
        + [array(parts, wide, part, dtype=BF16)] * 2
        + [array(part // LANES * n, LANES) for n in samples],
        grid_spec=pltpu.PrefetchScalarGridSpec(
            num_scalar_prefetch=1,
            grid=(parts,),
            in_specs=[pl.BlockSpec((CUBE, part, cols), lambda j, at: (0, j + first, 0))]
            + [pl.BlockSpec((n, part), lambda j, at: (0, at[0])) for n in samples],
            out_specs=[WHOLE] * (4 + len(samples)),
        ),
        compiler_params=pltpu.CompilerParams(vmem_limit_bytes=12 << 20),
    )(at, in_hbm(jacobian), *(in_hbm(t) for t in targets))


def beside_kernel(own_ref, other_ref, out_ref):
    members = own_ref.shape[0]
    out_ref[:members] = own_ref[...]
    out_ref[members:] = other_ref[...]


def beside(own, other):
    shape = (2 * own.shape[0], *own.shape[1:])
    return call(beside_kernel, array(*shape), "beside", 4, in_specs=[WHOLE] * 2, out_specs=WHOLE)(own, other)


def across(bit):
    pairs = []
    for group in SECOND:
        for k in range(CUBE):
            corner = corner_of(k) ^ (1 << bit)
            pairs.append((group[k], group[number((corner >> 2, corner >> 1 & 1, corner & 1))]))
    return pairs


def open_kernel(at_ref, theta_ref, *refs):
    flips, (out_ref, both_ref) = refs[:-2], refs[-2:]
    samples, cols = theta_ref.shape[1:]
    for c in range(CUBE):
        theta = theta_ref[corner_of(c) ^ at_ref[1]]
        both_ref[:, c * cols : (c + 1) * cols], _ = stacked(theta)
    both = both_ref[...]
    put_all(out_ref, both, both[:samples], flips, jnp.zeros((TAIL, LANES), F32))


def put_all(out_ref, both, high, flips, tail):
    j = 0
    for high_ref, low_ref in zip(flips[::2], flips[1::2]):
        for k in range(high_ref.shape[0]):
            put_part(out_ref, j, both, high, high_ref[k], low_ref[k], tail)
            j += 1


def opened(at, theta, flips):
    samples, cols = theta.shape[1:]
    length = flips[0].shape[2] // LANES * samples
    return call(
        open_kernel,
        array(CUBE, length + TAIL, LANES),
        "opened",
        6,
        in_specs=[pl.BlockSpec(memory_space=pltpu.SMEM)] + [WHOLE] * (1 + len(flips)),
        out_specs=WHOLE,
        scratch_shapes=[pltpu.VMEM((2 * samples, CUBE * cols), BF16)],
    )(at, theta, *flips)


def in_hbm(x):
    return pltpu.with_memory_space_constraint(x, pltpu.HBM)


def fold_kernel(in_ref, out_ref):
    out_ref[...] = jnp.sum(in_ref[...], axis=0)


def fold(parts):
    return call(fold_kernel, array(*parts.shape[1:]), "fold", 4, in_specs=[WHOLE], out_specs=WHOLE)(parts)


def scale_from(row, samples, clip_level, params):
    squares = to_column(row, samples)
    return jnp.minimum(1.0, clip_level / jnp.sqrt(squares / params + 1e-06))


def residual_to(out_ref, logits, targets):
    residual = jax.nn.sigmoid(logits) - targets
    for i in range(CUBE):
        out_ref[i] = residual


def first_residual_kernel(in_ref, targets_ref, residual_ref, logits_ref):
    logits = jnp.sum(in_ref[:, : targets_ref.shape[0]], axis=0)
    logits_ref[...] = logits
    residual_to(residual_ref, logits, targets_ref[...])


def first_residual(parts, targets):
    return call(
        first_residual_kernel,
        [array(CUBE, *targets.shape), array(*targets.shape)],
        "first_residual",
        4,
        in_specs=[WHOLE] * 2,
        out_specs=[WHOLE] * 2,
    )(parts, targets)


def next_residual(parts, targets, logits, slope, samples, clip_level, params, last):
    def kernel(in_ref, targets_ref, logits_ref, slope_ref, residual_ref, scale_ref, *kept):
        length = targets_ref.shape[0]
        row = jnp.sum(in_ref[:, length:], axis=0)[:1]
        scale = scale_from(row, samples, clip_level, params)
        scale_ref[...] = jnp.broadcast_to(scale, scale_ref.shape)
        moved = jnp.sum(in_ref[:, :length], axis=0)
        every = jnp.concatenate([scale] * (length // samples), 0)
        slope = 0.9 * slope_ref[...] + every * moved
        logits = logits_ref[...] - 0.5 * slope
        if kept:
            kept[0][...] = logits
            kept[1][...] = slope
        residual_to(residual_ref, logits, targets_ref[...])

    shape = targets.shape
    kept = 0 if last else 2
    return call(
        kernel,
        [array(CUBE, *shape), array(samples, LANES)] + [array(*shape)] * kept,
        "last_residual" if last else "next_residual",
        4,
        in_specs=[WHOLE] * 4,
        out_specs=[WHOLE] * (2 + kept),
    )(parts, targets, logits, slope)


def joined(in_ref, samples):
    blocks, length = in_ref.shape[0], in_ref.shape[1] // samples * samples
    return jnp.concatenate([in_ref[b, t : t + samples] for b in range(blocks) for t in range(0, length, samples)], 1)


def gradient_kernel(residual_ref, *refs):
    jac, out_ref = refs[:-1], refs[-1]
    samples, cols = out_ref.shape[1:]
    both, high = stacked(joined(residual_ref, samples))
    for c in range(CUBE):
        at = slice(c * cols, (c + 1) * cols)
        total, row = 0.0, 0
        for high_ref, low_ref in zip(jac[::2], jac[1::2]):
            rows = slice(row, row + high_ref.shape[0])
            wide = dot(both[:, rows], high_ref[:, at], DOWN)
            total += wide[:samples] + wide[samples:] + dot(high[:, rows], low_ref[:, at], DOWN)
            row = rows.stop
        out_ref[c] = total


def gradient_parts(residual, jac, samples):
    return call(
        gradient_kernel,
        array(CUBE, samples, jac[0].shape[1] // CUBE),
        "gradient",
        6,
        in_specs=[WHOLE] * (1 + len(jac)),
        out_specs=WHOLE,
    )(residual, *jac)


def moved_on(state):
    theta_ref, velocity_ref, gradient_ref, scale_ref = state
    velocity = 0.9 * velocity_ref[...] + scale_ref[:, :1] * gradient_ref[...]
    return theta_ref[...] - 0.5 * velocity, velocity


def whole_gradient(own_ref, other_ref, prec_ref, anchor_ref, theta):
    gradient = own_ref[...] + other_ref[...] + prec_ref[...] * (theta - anchor_ref[...])
    return gradient, jnp.sum(gradient * gradient, axis=1, keepdims=True)


def send_gradient(out_ref, gradient, square):
    samples, cols = gradient.shape
    tail = to_lanes(square)
    for c in range(CUBE):
        for t in range(cols // LANES):
            out_ref[c, t * samples : (t + 1) * samples] = gradient[:, t * LANES : (t + 1) * LANES]
        out_ref[c, cols // LANES * samples :] = tail


def first_step_kernel(own_ref, other_ref, prec_ref, anchor_ref, out_ref, gradient_ref):
    gradient, square = whole_gradient(own_ref, other_ref, prec_ref, anchor_ref, anchor_ref[...])
    gradient_ref[...] = gradient
    send_gradient(out_ref, gradient, square)


def next_step_kernel(own_ref, other_ref, prec_ref, anchor_ref, *refs):
    state, (out_ref, gradient_ref, theta_ref, velocity_ref) = refs[:4], refs[4:]
    theta, velocity = moved_on(state)
    theta_ref[...] = theta
    velocity_ref[...] = velocity
    gradient, square = whole_gradient(own_ref, other_ref, prec_ref, anchor_ref, theta)
    gradient_ref[...] = gradient
    send_gradient(out_ref, gradient, square)


def stepped(own, other, prec, anchor, state=()):
    samples, cols = anchor.shape
    outs = 3 if state else 1
    return call(
        next_step_kernel if state else first_step_kernel,
        [array(CUBE, cols // LANES * samples + TAIL, LANES)] + [array(samples, cols)] * outs,
        "next_step" if state else "first_step",
        4,
        in_specs=[WHOLE] * (4 + len(state)),
        out_specs=[WHOLE] * (1 + outs),
    )(own, other, prec, anchor, *state)


def push(parts, flips, samples):
    def kernel(in_ref, *refs):
        both, first = stacked(joined(in_ref, samples))
        put_all(refs[-1], both, first, refs[:-1], jnp.sum(in_ref[:, -TAIL:], axis=0))

    return call(
        kernel,
        array(CUBE, flips[0].shape[2] // LANES * samples + TAIL, LANES),
        "push",
        6,
        in_specs=[WHOLE] * (1 + len(flips)),
        out_specs=WHOLE,
    )(parts, *flips)


def last_kernel(own_ref, other_ref, prec_ref, anchor_ref, *refs):
    state, (squares_ref, gradient_ref, theta_ref, velocity_ref) = refs[:4], refs[4:]
    theta, velocity = moved_on(state)
    theta_ref[...] = theta
    velocity_ref[...] = velocity
    gradient, square = whole_gradient(own_ref, other_ref, prec_ref, anchor_ref, theta)
    gradient_ref[...] = gradient
    squares_ref[...] = jnp.broadcast_to(to_lanes(square)[:1], squares_ref.shape)


def last_gradient(own, other, prec, anchor, state):
    shape = anchor.shape
    return call(
        last_kernel,
        [array(SIDE**3, LANES)] + [array(*shape)] * 3,
        "last_gradient",
        4,
        in_specs=[WHOLE] * 8,
        out_specs=[WHOLE] * 4,
    )(own, other, prec, anchor, *state)


def close(squares, theta, velocity, gradient, clip_level, params):
    samples = theta.shape[0]

    def kernel(squares_ref, theta_ref, velocity_ref, gradient_ref, out_ref):
        row = jnp.sum(squares_ref[...], axis=0, keepdims=True)
        scale = scale_from(row, samples, clip_level, params)
        velocity = 0.9 * velocity_ref[...] + scale * gradient_ref[...]
        out_ref[...] = theta_ref[...] - 0.5 * velocity

    return call(kernel, array(*theta.shape), "close", 4, in_specs=[WHOLE] * 4, out_specs=WHOLE)(
        squares, theta, velocity, gradient
    )


def body(jacobian, targets, anchor, precision):
    samples, col_dev = anchor.shape
    row_dev = jacobian.shape[0]
    params = col_dev * SIDE**3
    clip_level = 0.2 * math.sqrt(row_dev * 2 / params)
    half, pair = own_block()
    at = jnp.stack([pair * CUBE + half, corner_of(pair)]).astype(jnp.int32)
    prec = precision[None, :]
    jacobian, at = lax.optimization_barrier((jacobian, at))
    square = exchange(jacobian.reshape(CUBE, row_dev // CUBE, col_dev), SECOND)
    square, theta = lax.optimization_barrier((square, anchor[None]))
    jac, flips, first = [], [], 0
    for bit, parts in enumerate(SPLIT):
        other = lax.ppermute(theta, AXES, across(bit))
        pieces = split(at, square, first, parts, () if bit else (targets,))
        other, square, high, low, *flip = lax.optimization_barrier((other, square, *pieces))
        if not bit:
            *flip, own = flip
        theta = beside(theta, other)
        jac, flips, first = [*jac, high, low], [*flips, *flip], first + parts
    parts = opened(at, theta, flips)
    residual, logits = first_residual(exchange(parts, FIRST), own)
    slope = jnp.zeros_like(logits)
    state = ()
    for step in range(STEPS):
        parts = gradient_parts(exchange(residual, FIRST), jac, samples)
        gradient = fold(exchange(parts, SECOND))
        other = lax.ppermute(gradient, "rows", [(0, 1), (1, 0)])
        if step + 1 == STEPS:
            break
        parts, gradient, *moved = stepped(gradient, other, prec, anchor, state)
        theta, velocity = moved if moved else (anchor, jnp.zeros_like(anchor))
        parts = exchange(push(exchange(parts, SECOND), flips, samples), FIRST)
        last = step + 2 == STEPS
        residual, scale, *kept = next_residual(parts, own, logits, slope, samples, clip_level, params, last)
        logits, slope = kept or (None, None)
        state = (theta, velocity, gradient, scale)
    squares, gradient, theta, velocity = last_gradient(gradient, other, prec, anchor, state)
    squares = lax.all_to_all(squares, COLS, split_axis=0, concat_axis=0, tiled=True)
    return close(squares, theta, velocity, gradient, clip_level, params)


def solution(mesh):
    cubes = Mesh(mesh.devices.reshape(2, SIDE, SIDE, SIDE), AXES)
    in_specs = (P("rows", COLS), P(None, "rows"), P(None, COLS), P(COLS))
    out_specs = P(None, COLS)
    return jax.shard_map(body, mesh=cubes, in_specs=in_specs, out_specs=out_specs, check_vma=False)
```

```python
import math

import jax
import jax.numpy as jnp
from jax import lax
from jax.experimental import pallas as pl
from jax.experimental.pallas import tpu as pltpu
from jax.sharding import Mesh
from jax.sharding import PartitionSpec as P

STEPS = 3
SPLIT = (2, 3, 3)
SIDE = 4
CUBE = 8
SHIFT = (1, 1, 0)
AXES = ("rows", "z", "y", "x")
COLS = ("z", "y", "x")
LANES = 128
TAIL = 8
F32 = jnp.float32
BF16 = jnp.bfloat16
ACROSS = (((1,), (1,)), ((), ()))
DOWN = (((1,), (0,)), ((), ()))
WHOLE = pl.BlockSpec(memory_space=pltpu.VMEM)


def place(core, at):
    turned = [(p + core + s) & (SIDE - 1) for p, s in zip(at, SHIFT)]
    half = [((t + 1) >> 1) & 1 for t in turned]
    pair = [t >> 1 for t in turned]
    return number(half), number(pair)


def number(bits):
    a, b, c = bits
    return (a ^ b) * 4 + (a ^ c) * 2 + a


def corner_of(k):
    return (k & 1) * 4 + ((k >> 1) ^ (3 * (k & 1)))


def cube_groups():
    first, second = {}, {}
    for device in range(2 * SIDE**3):
        core, z, y, x = device // 64, device // 16 % 4, device // 4 % 4, device % 4
        half, pair = place(core, (z, y, x))
        first.setdefault((core, pair), {})[half] = device
        second.setdefault((core, half), {})[pair] = device
    in_order = lambda groups: [[group[k] for k in range(CUBE)] for _, group in sorted(groups.items())]
    return in_order(first), in_order(second)


def everyone():
    pairs = []
    for chip in range(SIDE**3 // 2):
        z, y, x = chip // 16, chip // 4 % 4, chip % 4
        pairs += [chip, (z ^ 2) * 16 + (y ^ 2) * 4 + (x ^ 2)]
    return [[core * SIDE**3 + chip for chip in pairs] for core in range(2)]


FIRST, SECOND = cube_groups()
ALL = everyone()


def exchange(x, groups):
    return lax.all_to_all(x, AXES, split_axis=0, concat_axis=0, axis_index_groups=groups, tiled=True)


def own_block():
    return place(lax.axis_index("rows"), [lax.axis_index(a) for a in COLS])


def call(kernel, out_shape, name, mib, **kw):
    return pl.pallas_call(
        kernel,
        out_shape=out_shape,
        name=name,
        compiler_params=pltpu.CompilerParams(vmem_limit_bytes=mib << 20),
        **kw,
    )


def array(*shape, dtype=F32):
    return jax.ShapeDtypeStruct(shape, dtype)


def halves(x):
    high = x.astype(BF16)
    return high, (x - high.astype(F32)).astype(BF16)


def dot(a, b, dims):
    return lax.dot_general(a, b, dims, preferred_element_type=F32)


def diagonal(samples):
    shape = (samples, LANES)
    return lax.broadcasted_iota(jnp.int32, shape, 0) == lax.broadcasted_iota(jnp.int32, shape, 1)


def to_lanes(column):
    samples = column.shape[0]
    row = jnp.sum(jnp.where(diagonal(samples), column, 0.0), axis=0, keepdims=True)
    return jnp.broadcast_to(row, (TAIL, LANES))


def to_column(row, samples):
    return jnp.sum(jnp.where(diagonal(samples), row, 0.0), axis=1, keepdims=True)


def stacked(x):
    high, low = halves(x)
    return jnp.concatenate([high, low], 0), high


def put_part(out_ref, j, both, high, flip_high, flip_low, tail):
    samples = high.shape[0]
    tiles = flip_high.shape[1] // LANES
    wide = dot(both, flip_high, DOWN)
    logits = wide[:samples] + wide[samples:] + dot(high, flip_low, DOWN)
    for t in range(tiles):
        out_ref[j, t * samples : (t + 1) * samples] = logits[:, t * LANES : (t + 1) * LANES]
    out_ref[j, tiles * samples :] = tail


def split_kernel(at_ref, jac_ref, *refs):
    if len(refs) > 4:
        targets_ref, *refs, own_ref = refs
        samples = targets_ref.shape[0]
        for t in range(targets_ref.shape[1] // LANES):
            own_ref[t * samples : (t + 1) * samples] = targets_ref[:, t * LANES : (t + 1) * LANES]
    high_ref, low_ref, flip_high_ref, flip_low_ref = refs
    j = pl.program_id(0)
    _, part, cols = jac_ref.shape
    rows = pl.ds(pl.multiple_of(j * part, part), part)
    for c in range(CUBE):
        jac_high, jac_low = halves(jac_ref[c])
        at = slice(c * cols, (c + 1) * cols)
        high_ref[rows, at] = jac_high
        low_ref[rows, at] = jac_low
        flip_high_ref[j, at] = jnp.transpose(jac_high)
        flip_low_ref[j, at] = jnp.transpose(jac_low)


def split(at, jacobian, first, parts, targets=()):
    _, rows, cols = jacobian.shape
    part = rows // CUBE
    wide = CUBE * cols
    samples = [t.shape[0] for t in targets]
    return pl.pallas_call(
        split_kernel,
        name="split",
        out_shape=[array(parts * part, wide, dtype=BF16)] * 2
        + [array(parts, wide, part, dtype=BF16)] * 2
        + [array(part // LANES * n, LANES) for n in samples],
        grid_spec=pltpu.PrefetchScalarGridSpec(
            num_scalar_prefetch=1,
            grid=(parts,),
            in_specs=[pl.BlockSpec((CUBE, part, cols), lambda j, at: (0, j + first, 0))]
            + [pl.BlockSpec((n, part), lambda j, at: (0, at[0])) for n in samples],
            out_specs=[WHOLE] * (4 + len(samples)),
        ),
        compiler_params=pltpu.CompilerParams(vmem_limit_bytes=12 << 20),
    )(at, in_hbm(jacobian), *(in_hbm(t) for t in targets))


def beside_kernel(own_ref, other_ref, out_ref):
    members = own_ref.shape[0]
    out_ref[:members] = own_ref[...]
    out_ref[members:] = other_ref[...]


def beside(own, other):
    shape = (2 * own.shape[0], *own.shape[1:])
    return call(beside_kernel, array(*shape), "beside", 4, in_specs=[WHOLE] * 2, out_specs=WHOLE)(own, other)


def across(bit):
    pairs = []
    for group in SECOND:
        for k in range(CUBE):
            corner = corner_of(k) ^ (1 << bit)
            pairs.append((group[k], group[number((corner >> 2, corner >> 1 & 1, corner & 1))]))
    return pairs


def open_kernel(at_ref, theta_ref, *refs):
    flips, (out_ref, both_ref) = refs[:-2], refs[-2:]
    samples, cols = theta_ref.shape[1:]
    for c in range(CUBE):
        theta = theta_ref[corner_of(c) ^ at_ref[1]]
        both_ref[:, c * cols : (c + 1) * cols], _ = stacked(theta)
    both = both_ref[...]
    put_all(out_ref, both, both[:samples], flips, jnp.zeros((TAIL, LANES), F32))


def put_all(out_ref, both, high, flips, tail):
    j = 0
    for high_ref, low_ref in zip(flips[::2], flips[1::2]):
        for k in range(high_ref.shape[0]):
            put_part(out_ref, j, both, high, high_ref[k], low_ref[k], tail)
            j += 1


def opened(at, theta, flips):
    samples, cols = theta.shape[1:]
    length = flips[0].shape[2] // LANES * samples
    return call(
        open_kernel,
        array(CUBE, length + TAIL, LANES),
        "opened",
        6,
        in_specs=[pl.BlockSpec(memory_space=pltpu.SMEM)] + [WHOLE] * (1 + len(flips)),
        out_specs=WHOLE,
        scratch_shapes=[pltpu.VMEM((2 * samples, CUBE * cols), BF16)],
    )(at, theta, *flips)


def in_hbm(x):
    return pltpu.with_memory_space_constraint(x, pltpu.HBM)


def fold_kernel(in_ref, out_ref):
    out_ref[...] = jnp.sum(in_ref[...], axis=0)


def fold(parts):
    return call(fold_kernel, array(*parts.shape[1:]), "fold", 4, in_specs=[WHOLE], out_specs=WHOLE)(parts)


def scale_from(row, samples, clip_level, params):
    squares = to_column(row, samples)
    return jnp.minimum(1.0, clip_level / jnp.sqrt(squares / params + 1e-06))


def residual_to(out_ref, logits, targets):
    residual = jax.nn.sigmoid(logits) - targets
    for i in range(CUBE):
        out_ref[i] = residual


def first_residual_kernel(in_ref, targets_ref, residual_ref, logits_ref):
    logits = jnp.sum(in_ref[:, : targets_ref.shape[0]], axis=0)
    logits_ref[...] = logits
    residual_to(residual_ref, logits, targets_ref[...])


def first_residual(parts, targets):
    return call(
        first_residual_kernel,
        [array(CUBE, *targets.shape), array(*targets.shape)],
        "first_residual",
        4,
        in_specs=[WHOLE] * 2,
        out_specs=[WHOLE] * 2,
    )(parts, targets)


def next_residual(parts, targets, logits, slope, samples, clip_level, params, last):
    def kernel(in_ref, targets_ref, logits_ref, slope_ref, residual_ref, scale_ref, *kept):
        length = targets_ref.shape[0]
        row = jnp.sum(in_ref[:, length:], axis=0)[:1]
        scale = scale_from(row, samples, clip_level, params)
        scale_ref[...] = jnp.broadcast_to(scale, scale_ref.shape)
        moved = jnp.sum(in_ref[:, :length], axis=0)
        every = jnp.concatenate([scale] * (length // samples), 0)
        slope = 0.9 * slope_ref[...] + every * moved
        logits = logits_ref[...] - 0.5 * slope
        if kept:
            kept[0][...] = logits
            kept[1][...] = slope
        residual_to(residual_ref, logits, targets_ref[...])

    shape = targets.shape
    kept = 0 if last else 2
    return call(
        kernel,
        [array(CUBE, *shape), array(samples, LANES)] + [array(*shape)] * kept,
        "last_residual" if last else "next_residual",
        4,
        in_specs=[WHOLE] * 4,
        out_specs=[WHOLE] * (2 + kept),
    )(parts, targets, logits, slope)


def joined(in_ref, samples):
    blocks, length = in_ref.shape[0], in_ref.shape[1] // samples * samples
    return jnp.concatenate([in_ref[b, t : t + samples] for b in range(blocks) for t in range(0, length, samples)], 1)


def gradient_kernel(residual_ref, *refs):
    jac, out_ref = refs[:-1], refs[-1]
    samples, cols = out_ref.shape[1:]
    both, high = stacked(joined(residual_ref, samples))
    for c in range(CUBE):
        at = slice(c * cols, (c + 1) * cols)
        total, row = 0.0, 0
        for high_ref, low_ref in zip(jac[::2], jac[1::2]):
            rows = slice(row, row + high_ref.shape[0])
            wide = dot(both[:, rows], high_ref[:, at], DOWN)
            total += wide[:samples] + wide[samples:] + dot(high[:, rows], low_ref[:, at], DOWN)
            row = rows.stop
        out_ref[c] = total


def gradient_parts(residual, jac, samples):
    return call(
        gradient_kernel,
        array(CUBE, samples, jac[0].shape[1] // CUBE),
        "gradient",
        6,
        in_specs=[WHOLE] * (1 + len(jac)),
        out_specs=WHOLE,
    )(residual, *jac)


def moved_on(state):
    theta_ref, velocity_ref, gradient_ref, scale_ref = state
    velocity = 0.9 * velocity_ref[...] + scale_ref[:, :1] * gradient_ref[...]
    return theta_ref[...] - 0.5 * velocity, velocity


def whole_gradient(own_ref, other_ref, prec_ref, anchor_ref, theta):
    gradient = own_ref[...] + other_ref[...] + prec_ref[...] * (theta - anchor_ref[...])
    return gradient, jnp.sum(gradient * gradient, axis=1, keepdims=True)


def send_gradient(out_ref, gradient, square):
    samples, cols = gradient.shape
    tail = to_lanes(square)
    for c in range(CUBE):
        for t in range(cols // LANES):
            out_ref[c, t * samples : (t + 1) * samples] = gradient[:, t * LANES : (t + 1) * LANES]
        out_ref[c, cols // LANES * samples :] = tail


def first_step_kernel(own_ref, other_ref, prec_ref, anchor_ref, out_ref, gradient_ref):
    gradient, square = whole_gradient(own_ref, other_ref, prec_ref, anchor_ref, anchor_ref[...])
    gradient_ref[...] = gradient
    send_gradient(out_ref, gradient, square)


def next_step_kernel(own_ref, other_ref, prec_ref, anchor_ref, *refs):
    state, (out_ref, gradient_ref, theta_ref, velocity_ref) = refs[:4], refs[4:]
    theta, velocity = moved_on(state)
    theta_ref[...] = theta
    velocity_ref[...] = velocity
    gradient, square = whole_gradient(own_ref, other_ref, prec_ref, anchor_ref, theta)
    gradient_ref[...] = gradient
    send_gradient(out_ref, gradient, square)


def stepped(own, other, prec, anchor, state=()):
    samples, cols = anchor.shape
    outs = 3 if state else 1
    return call(
        next_step_kernel if state else first_step_kernel,
        [array(CUBE, cols // LANES * samples + TAIL, LANES)] + [array(samples, cols)] * outs,
        "next_step" if state else "first_step",
        4,
        in_specs=[WHOLE] * (4 + len(state)),
        out_specs=[WHOLE] * (1 + outs),
    )(own, other, prec, anchor, *state)


def push(parts, flips, samples):
    def kernel(in_ref, *refs):
        both, first = stacked(joined(in_ref, samples))
        put_all(refs[-1], both, first, refs[:-1], jnp.sum(in_ref[:, -TAIL:], axis=0))

    return call(
        kernel,
        array(CUBE, flips[0].shape[2] // LANES * samples + TAIL, LANES),
        "push",
        6,
        in_specs=[WHOLE] * (1 + len(flips)),
        out_specs=WHOLE,
    )(parts, *flips)


def last_kernel(own_ref, other_ref, prec_ref, anchor_ref, *refs):
    state, (squares_ref, gradient_ref, theta_ref, velocity_ref) = refs[:4], refs[4:]
    theta, velocity = moved_on(state)
    theta_ref[...] = theta
    velocity_ref[...] = velocity
    gradient, square = whole_gradient(own_ref, other_ref, prec_ref, anchor_ref, theta)
    gradient_ref[...] = gradient
    squares_ref[...] = jnp.broadcast_to(to_lanes(square)[:1], squares_ref.shape)


def last_gradient(own, other, prec, anchor, state):
    shape = anchor.shape
    return call(
        last_kernel,
        [array(SIDE**3, LANES)] + [array(*shape)] * 3,
        "last_gradient",
        4,
        in_specs=[WHOLE] * 8,
        out_specs=[WHOLE] * 4,
    )(own, other, prec, anchor, *state)


def close(squares, theta, velocity, gradient, clip_level, params):
    samples = theta.shape[0]

    def kernel(squares_ref, theta_ref, velocity_ref, gradient_ref, out_ref):
        row = jnp.sum(squares_ref[...], axis=0, keepdims=True)
        scale = scale_from(row, samples, clip_level, params)
        velocity = 0.9 * velocity_ref[...] + scale * gradient_ref[...]
        out_ref[...] = theta_ref[...] - 0.5 * velocity

    return call(kernel, array(*theta.shape), "close", 4, in_specs=[WHOLE] * 4, out_specs=WHOLE)(
        squares, theta, velocity, gradient
    )


def body(jacobian, targets, anchor, precision):
    samples, col_dev = anchor.shape
    row_dev = jacobian.shape[0]
    params = col_dev * SIDE**3
    clip_level = 0.2 * math.sqrt(row_dev * 2 / params)
    half, pair = own_block()
    at = jnp.stack([pair * CUBE + half, corner_of(pair)]).astype(jnp.int32)
    prec = precision[None, :]
    jacobian, at = lax.optimization_barrier((jacobian, at))
    square = exchange(jacobian.reshape(CUBE, row_dev // CUBE, col_dev), SECOND)
    square, theta = lax.optimization_barrier((square, anchor[None]))
    jac, flips, first = [], [], 0
    for bit, parts in enumerate(SPLIT):
        other = lax.ppermute(theta, AXES, across(bit))
        pieces = split(at, square, first, parts, () if bit else (targets,))
        other, square, high, low, *flip = lax.optimization_barrier((other, square, *pieces))
        if not bit:
            *flip, own = flip
        theta = beside(theta, other)
        jac, flips, first = [*jac, high, low], [*flips, *flip], first + parts
    parts = opened(at, theta, flips)
    residual, logits = first_residual(exchange(parts, FIRST), own)
    slope = jnp.zeros_like(logits)
    state = ()
    for step in range(STEPS):
        parts = gradient_parts(exchange(residual, FIRST), jac, samples)
        gradient = fold(exchange(parts, SECOND))
        other = lax.ppermute(gradient, "rows", [(0, 1), (1, 0)])
        if step + 1 == STEPS:
            break
        parts, gradient, *moved = stepped(gradient, other, prec, anchor, state)
        theta, velocity = moved if moved else (anchor, jnp.zeros_like(anchor))
        parts = exchange(push(exchange(parts, SECOND), flips, samples), FIRST)
        last = step + 2 == STEPS
        residual, scale, *kept = next_residual(parts, own, logits, slope, samples, clip_level, params, last)
        logits, slope = kept or (None, None)
        state = (theta, velocity, gradient, scale)
    squares, gradient, theta, velocity = last_gradient(gradient, other, prec, anchor, state)
    squares = exchange(squares, ALL)
    return close(squares, theta, velocity, gradient, clip_level, params)


def solution(mesh):
    cubes = Mesh(mesh.devices.reshape(2, SIDE, SIDE, SIDE), AXES)
    in_specs = (P("rows", COLS), P(None, "rows"), P(None, COLS), P(COLS))
    out_specs = P(None, COLS)
    return jax.shard_map(body, mesh=cubes, in_specs=in_specs, out_specs=out_specs, check_vma=False)
```

```python
import math

import jax
import jax.numpy as jnp
from jax import lax
from jax.experimental import pallas as pl
from jax.experimental.pallas import tpu as pltpu
from jax.sharding import Mesh
from jax.sharding import PartitionSpec as P

STEPS = 3
SPLIT = (2, 2, 4)
SIDE = 4
CUBE = 8
SHIFT = (1, 1, 0)
AXES = ("rows", "z", "y", "x")
COLS = ("z", "y", "x")
LANES = 128
TAIL = 8
F32 = jnp.float32
BF16 = jnp.bfloat16
ACROSS = (((1,), (1,)), ((), ()))
DOWN = (((1,), (0,)), ((), ()))
WHOLE = pl.BlockSpec(memory_space=pltpu.VMEM)


def place(core, at):
    turned = [(p + core + s) & (SIDE - 1) for p, s in zip(at, SHIFT)]
    half = [((t + 1) >> 1) & 1 for t in turned]
    pair = [t >> 1 for t in turned]
    return number(half), number(pair)


def number(bits):
    a, b, c = bits
    return (a ^ b) * 4 + (a ^ c) * 2 + a


def corner_of(k):
    return (k & 1) * 4 + ((k >> 1) ^ (3 * (k & 1)))


def cube_groups():
    first, second = {}, {}
    for device in range(2 * SIDE**3):
        core, z, y, x = device // 64, device // 16 % 4, device // 4 % 4, device % 4
        half, pair = place(core, (z, y, x))
        first.setdefault((core, pair), {})[half] = device
        second.setdefault((core, half), {})[pair] = device
    in_order = lambda groups: [[group[k] for k in range(CUBE)] for _, group in sorted(groups.items())]
    return in_order(first), in_order(second)


def everyone():
    pairs = []
    for chip in range(SIDE**3 // 2):
        z, y, x = chip // 16, chip // 4 % 4, chip % 4
        pairs += [chip, (z ^ 2) * 16 + (y ^ 2) * 4 + (x ^ 2)]
    return [[core * SIDE**3 + chip for chip in pairs] for core in range(2)]


FIRST, SECOND = cube_groups()
ALL = everyone()


def exchange(x, groups):
    return lax.all_to_all(x, AXES, split_axis=0, concat_axis=0, axis_index_groups=groups, tiled=True)


def own_block():
    return place(lax.axis_index("rows"), [lax.axis_index(a) for a in COLS])


def call(kernel, out_shape, name, mib, **kw):
    return pl.pallas_call(
        kernel,
        out_shape=out_shape,
        name=name,
        compiler_params=pltpu.CompilerParams(vmem_limit_bytes=mib << 20),
        **kw,
    )


def array(*shape, dtype=F32):
    return jax.ShapeDtypeStruct(shape, dtype)


def halves(x):
    high = x.astype(BF16)
    return high, (x - high.astype(F32)).astype(BF16)


def dot(a, b, dims):
    return lax.dot_general(a, b, dims, preferred_element_type=F32)


def diagonal(samples):
    shape = (samples, LANES)
    return lax.broadcasted_iota(jnp.int32, shape, 0) == lax.broadcasted_iota(jnp.int32, shape, 1)


def to_lanes(column):
    samples = column.shape[0]
    row = jnp.sum(jnp.where(diagonal(samples), column, 0.0), axis=0, keepdims=True)
    return jnp.broadcast_to(row, (TAIL, LANES))


def to_column(row, samples):
    return jnp.sum(jnp.where(diagonal(samples), row, 0.0), axis=1, keepdims=True)


def stacked(x):
    high, low = halves(x)
    return jnp.concatenate([high, low], 0), high


def put_part(out_ref, j, both, high, flip_high, flip_low, tail):
    samples = high.shape[0]
    tiles = flip_high.shape[1] // LANES
    wide = dot(both, flip_high, DOWN)
    logits = wide[:samples] + wide[samples:] + dot(high, flip_low, DOWN)
    for t in range(tiles):
        out_ref[j, t * samples : (t + 1) * samples] = logits[:, t * LANES : (t + 1) * LANES]
    out_ref[j, tiles * samples :] = tail


def split_kernel(at_ref, jac_ref, *refs):
    if len(refs) > 4:
        targets_ref, *refs, own_ref = refs
        samples = targets_ref.shape[0]
        for t in range(targets_ref.shape[1] // LANES):
            own_ref[t * samples : (t + 1) * samples] = targets_ref[:, t * LANES : (t + 1) * LANES]
    high_ref, low_ref, flip_high_ref, flip_low_ref = refs
    j = pl.program_id(0)
    _, part, cols = jac_ref.shape
    rows = pl.ds(pl.multiple_of(j * part, part), part)
    for c in range(CUBE):
        jac_high, jac_low = halves(jac_ref[c])
        at = slice(c * cols, (c + 1) * cols)
        high_ref[rows, at] = jac_high
        low_ref[rows, at] = jac_low
        flip_high_ref[j, at] = jnp.transpose(jac_high)
        flip_low_ref[j, at] = jnp.transpose(jac_low)


def split(at, jacobian, first, parts, targets=()):
    _, rows, cols = jacobian.shape
    part = rows // CUBE
    wide = CUBE * cols
    samples = [t.shape[0] for t in targets]
    return pl.pallas_call(
        split_kernel,
        name="split",
        out_shape=[array(parts * part, wide, dtype=BF16)] * 2
        + [array(parts, wide, part, dtype=BF16)] * 2
        + [array(part // LANES * n, LANES) for n in samples],
        grid_spec=pltpu.PrefetchScalarGridSpec(
            num_scalar_prefetch=1,
            grid=(parts,),
            in_specs=[pl.BlockSpec((CUBE, part, cols), lambda j, at: (0, j + first, 0))]
            + [pl.BlockSpec((n, part), lambda j, at: (0, at[0])) for n in samples],
            out_specs=[WHOLE] * (4 + len(samples)),
        ),
        compiler_params=pltpu.CompilerParams(vmem_limit_bytes=12 << 20),
    )(at, in_hbm(jacobian), *(in_hbm(t) for t in targets))


def beside_kernel(own_ref, other_ref, out_ref):
    members = own_ref.shape[0]
    out_ref[:members] = own_ref[...]
    out_ref[members:] = other_ref[...]


def beside(own, other):
    shape = (2 * own.shape[0], *own.shape[1:])
    return call(beside_kernel, array(*shape), "beside", 4, in_specs=[WHOLE] * 2, out_specs=WHOLE)(own, other)


def across(bit):
    pairs = []
    for group in SECOND:
        for k in range(CUBE):
            corner = corner_of(k) ^ (1 << bit)
            pairs.append((group[k], group[number((corner >> 2, corner >> 1 & 1, corner & 1))]))
    return pairs


def open_kernel(at_ref, theta_ref, *refs):
    flips, (out_ref, both_ref) = refs[:-2], refs[-2:]
    samples, cols = theta_ref.shape[1:]
    for c in range(CUBE):
        theta = theta_ref[corner_of(c) ^ at_ref[1]]
        both_ref[:, c * cols : (c + 1) * cols], _ = stacked(theta)
    both = both_ref[...]
    put_all(out_ref, both, both[:samples], flips, jnp.zeros((TAIL, LANES), F32))


def put_all(out_ref, both, high, flips, tail):
    j = 0
    for high_ref, low_ref in zip(flips[::2], flips[1::2]):
        for k in range(high_ref.shape[0]):
            put_part(out_ref, j, both, high, high_ref[k], low_ref[k], tail)
            j += 1


def opened(at, theta, flips):
    samples, cols = theta.shape[1:]
    length = flips[0].shape[2] // LANES * samples
    return call(
        open_kernel,
        array(CUBE, length + TAIL, LANES),
        "opened",
        6,
        in_specs=[pl.BlockSpec(memory_space=pltpu.SMEM)] + [WHOLE] * (1 + len(flips)),
        out_specs=WHOLE,
        scratch_shapes=[pltpu.VMEM((2 * samples, CUBE * cols), BF16)],
    )(at, theta, *flips)


def in_hbm(x):
    return pltpu.with_memory_space_constraint(x, pltpu.HBM)


def fold_kernel(in_ref, out_ref):
    out_ref[...] = jnp.sum(in_ref[...], axis=0)


def fold(parts):
    return call(fold_kernel, array(*parts.shape[1:]), "fold", 4, in_specs=[WHOLE], out_specs=WHOLE)(parts)


def scale_from(row, samples, clip_level, params):
    squares = to_column(row, samples)
    return jnp.minimum(1.0, clip_level / jnp.sqrt(squares / params + 1e-06))


def residual_to(out_ref, logits, targets):
    residual = jax.nn.sigmoid(logits) - targets
    for i in range(CUBE):
        out_ref[i] = residual


def first_residual_kernel(in_ref, targets_ref, residual_ref, logits_ref):
    logits = jnp.sum(in_ref[:, : targets_ref.shape[0]], axis=0)
    logits_ref[...] = logits
    residual_to(residual_ref, logits, targets_ref[...])


def first_residual(parts, targets):
    return call(
        first_residual_kernel,
        [array(CUBE, *targets.shape), array(*targets.shape)],
        "first_residual",
        4,
        in_specs=[WHOLE] * 2,
        out_specs=[WHOLE] * 2,
    )(parts, targets)


def next_residual(parts, targets, logits, slope, samples, clip_level, params, last):
    def kernel(in_ref, targets_ref, logits_ref, slope_ref, residual_ref, scale_ref, *kept):
        length = targets_ref.shape[0]
        row = jnp.sum(in_ref[:, length:], axis=0)[:1]
        scale = scale_from(row, samples, clip_level, params)
        scale_ref[...] = jnp.broadcast_to(scale, scale_ref.shape)
        moved = jnp.sum(in_ref[:, :length], axis=0)
        every = jnp.concatenate([scale] * (length // samples), 0)
        slope = 0.9 * slope_ref[...] + every * moved
        logits = logits_ref[...] - 0.5 * slope
        if kept:
            kept[0][...] = logits
            kept[1][...] = slope
        residual_to(residual_ref, logits, targets_ref[...])

    shape = targets.shape
    kept = 0 if last else 2
    return call(
        kernel,
        [array(CUBE, *shape), array(samples, LANES)] + [array(*shape)] * kept,
        "last_residual" if last else "next_residual",
        4,
        in_specs=[WHOLE] * 4,
        out_specs=[WHOLE] * (2 + kept),
    )(parts, targets, logits, slope)


def joined(in_ref, samples):
    blocks, length = in_ref.shape[0], in_ref.shape[1] // samples * samples
    return jnp.concatenate([in_ref[b, t : t + samples] for b in range(blocks) for t in range(0, length, samples)], 1)


def gradient_kernel(residual_ref, *refs):
    jac, out_ref = refs[:-1], refs[-1]
    samples, cols = out_ref.shape[1:]
    both, high = stacked(joined(residual_ref, samples))
    for c in range(CUBE):
        at = slice(c * cols, (c + 1) * cols)
        total, row = 0.0, 0
        for high_ref, low_ref in zip(jac[::2], jac[1::2]):
            rows = slice(row, row + high_ref.shape[0])
            wide = dot(both[:, rows], high_ref[:, at], DOWN)
            total += wide[:samples] + wide[samples:] + dot(high[:, rows], low_ref[:, at], DOWN)
            row = rows.stop
        out_ref[c] = total


def gradient_parts(residual, jac, samples):
    return call(
        gradient_kernel,
        array(CUBE, samples, jac[0].shape[1] // CUBE),
        "gradient",
        6,
        in_specs=[WHOLE] * (1 + len(jac)),
        out_specs=WHOLE,
    )(residual, *jac)


def moved_on(state):
    theta_ref, velocity_ref, gradient_ref, scale_ref = state
    velocity = 0.9 * velocity_ref[...] + scale_ref[:, :1] * gradient_ref[...]
    return theta_ref[...] - 0.5 * velocity, velocity


def whole_gradient(own_ref, other_ref, prec_ref, anchor_ref, theta):
    gradient = own_ref[...] + other_ref[...] + prec_ref[...] * (theta - anchor_ref[...])
    return gradient, jnp.sum(gradient * gradient, axis=1, keepdims=True)


def send_gradient(out_ref, gradient, square):
    samples, cols = gradient.shape
    tail = to_lanes(square)
    for c in range(CUBE):
        for t in range(cols // LANES):
            out_ref[c, t * samples : (t + 1) * samples] = gradient[:, t * LANES : (t + 1) * LANES]
        out_ref[c, cols // LANES * samples :] = tail


def first_step_kernel(own_ref, other_ref, prec_ref, anchor_ref, out_ref, gradient_ref):
    gradient, square = whole_gradient(own_ref, other_ref, prec_ref, anchor_ref, anchor_ref[...])
    gradient_ref[...] = gradient
    send_gradient(out_ref, gradient, square)


def next_step_kernel(own_ref, other_ref, prec_ref, anchor_ref, *refs):
    state, (out_ref, gradient_ref, theta_ref, velocity_ref) = refs[:4], refs[4:]
    theta, velocity = moved_on(state)
    theta_ref[...] = theta
    velocity_ref[...] = velocity
    gradient, square = whole_gradient(own_ref, other_ref, prec_ref, anchor_ref, theta)
    gradient_ref[...] = gradient
    send_gradient(out_ref, gradient, square)


def stepped(own, other, prec, anchor, state=()):
    samples, cols = anchor.shape
    outs = 3 if state else 1
    return call(
        next_step_kernel if state else first_step_kernel,
        [array(CUBE, cols // LANES * samples + TAIL, LANES)] + [array(samples, cols)] * outs,
        "next_step" if state else "first_step",
        4,
        in_specs=[WHOLE] * (4 + len(state)),
        out_specs=[WHOLE] * (1 + outs),
    )(own, other, prec, anchor, *state)


def push(parts, flips, samples):
    def kernel(in_ref, *refs):
        both, first = stacked(joined(in_ref, samples))
        put_all(refs[-1], both, first, refs[:-1], jnp.sum(in_ref[:, -TAIL:], axis=0))

    return call(
        kernel,
        array(CUBE, flips[0].shape[2] // LANES * samples + TAIL, LANES),
        "push",
        6,
        in_specs=[WHOLE] * (1 + len(flips)),
        out_specs=WHOLE,
    )(parts, *flips)


def last_kernel(own_ref, other_ref, prec_ref, anchor_ref, *refs):
    state, (squares_ref, gradient_ref, theta_ref, velocity_ref) = refs[:4], refs[4:]
    theta, velocity = moved_on(state)
    theta_ref[...] = theta
    velocity_ref[...] = velocity
    gradient, square = whole_gradient(own_ref, other_ref, prec_ref, anchor_ref, theta)
    gradient_ref[...] = gradient
    squares_ref[...] = jnp.broadcast_to(to_lanes(square)[:1], squares_ref.shape)


def last_gradient(own, other, prec, anchor, state):
    shape = anchor.shape
    return call(
        last_kernel,
        [array(SIDE**3, LANES)] + [array(*shape)] * 3,
        "last_gradient",
        4,
        in_specs=[WHOLE] * 8,
        out_specs=[WHOLE] * 4,
    )(own, other, prec, anchor, *state)


def close(squares, theta, velocity, gradient, clip_level, params):
    samples = theta.shape[0]

    def kernel(squares_ref, theta_ref, velocity_ref, gradient_ref, out_ref):
        row = jnp.sum(squares_ref[...], axis=0, keepdims=True)
        scale = scale_from(row, samples, clip_level, params)
        velocity = 0.9 * velocity_ref[...] + scale * gradient_ref[...]
        out_ref[...] = theta_ref[...] - 0.5 * velocity

    return call(kernel, array(*theta.shape), "close", 4, in_specs=[WHOLE] * 4, out_specs=WHOLE)(
        squares, theta, velocity, gradient
    )


def body(jacobian, targets, anchor, precision):
    samples, col_dev = anchor.shape
    row_dev = jacobian.shape[0]
    params = col_dev * SIDE**3
    clip_level = 0.2 * math.sqrt(row_dev * 2 / params)
    half, pair = own_block()
    at = jnp.stack([pair * CUBE + half, corner_of(pair)]).astype(jnp.int32)
    prec = precision[None, :]
    jacobian, at = lax.optimization_barrier((jacobian, at))
    square = exchange(jacobian.reshape(CUBE, row_dev // CUBE, col_dev), SECOND)
    square, theta = lax.optimization_barrier((square, anchor[None]))
    jac, flips, first = [], [], 0
    for bit, parts in enumerate(SPLIT):
        other = lax.ppermute(theta, AXES, across(bit))
        pieces = split(at, square, first, parts, () if bit else (targets,))
        other, square, high, low, *flip = lax.optimization_barrier((other, square, *pieces))
        if not bit:
            *flip, own = flip
        theta = beside(theta, other)
        jac, flips, first = [*jac, high, low], [*flips, *flip], first + parts
    parts = opened(at, theta, flips)
    residual, logits = first_residual(exchange(parts, FIRST), own)
    slope = jnp.zeros_like(logits)
    state = ()
    for step in range(STEPS):
        parts = gradient_parts(exchange(residual, FIRST), jac, samples)
        gradient = fold(exchange(parts, SECOND))
        other = lax.ppermute(gradient, "rows", [(0, 1), (1, 0)])
        if step + 1 == STEPS:
            break
        parts, gradient, *moved = stepped(gradient, other, prec, anchor, state)
        theta, velocity = moved if moved else (anchor, jnp.zeros_like(anchor))
        parts = exchange(push(exchange(parts, SECOND), flips, samples), FIRST)
        last = step + 2 == STEPS
        residual, scale, *kept = next_residual(parts, own, logits, slope, samples, clip_level, params, last)
        logits, slope = kept or (None, None)
        state = (theta, velocity, gradient, scale)
    squares, gradient, theta, velocity = last_gradient(gradient, other, prec, anchor, state)
    squares = exchange(squares, ALL)
    return close(squares, theta, velocity, gradient, clip_level, params)


def solution(mesh):
    cubes = Mesh(mesh.devices.reshape(2, SIDE, SIDE, SIDE), AXES)
    in_specs = (P("rows", COLS), P(None, "rows"), P(None, COLS), P(COLS))
    out_specs = P(None, COLS)
    return jax.shard_map(body, mesh=cubes, in_specs=in_specs, out_specs=out_specs, check_vma=False)
```
